32 devices in a mesh: row: 4 (over x, core), col: 8 (over z, y).
Axes of the slice: x: 2, y: 2, z: 4, core: 2. Of those that a mesh axis runs over, the one named last changes fastest.
Arguments:
- design: bfloat16 [512, 14080], P('row', 'col'), may hold values from -0.25 to 0.25
- nuisance_vals: float32 [4, 512], P(None, 'row'), may hold values from -2 to 2
- arc_index: int32 [512], P('row'), may hold values from 0 to 63, never falling along the last dimension, each value on 1 to 16 neighbouring positions
- filter_taps: float32 [128], replicated, may hold values from -0.5 to 0.5
- ordering: int32 [14336], replicated, may hold values from 0 to 14335, each once
- normal_prior: float32 [14336, 14336], P('row', 'col'), may hold values from -0.4 to 25
Outputs:
- normal_post: float32 [14336, 14336], P('row', 'col')
The draws below stay inside these ranges and needn't reach their ends.
Inputs may be any that keep to these rules, and one draw needn't show every extreme that they name: `arc_index`: arc numbers never fall along the rows; each arc covers 1 to 16 rows. `ordering`: every slot is the image of exactly one design column.
All inputs are finite; a program needn't handle non-finite values.
Results may differ from the reference program's by a relative error of at most 0.0065.
Values may be sent and summed in bfloat16 or wider, within the bound.
No kernel may reach another device: no remote copies, remote signals or barrier semaphores. Data moves between devices by JAX's collectives and lax.ppermute only.
A program may use at most 128 MiB of HBM per device.

```python
import math
import jax
import jax.numpy as jnp
import numpy as np
from jax import lax

COEF = 14080
NPA = 4
NARC = 64
LAG = 128
NUIS = 256
P_SIZE = 14336
OBS = 512


def draw_normal_prior(key, part):
    base = jax.random.fold_in(key, 7001)
    key_off, key_diag = jax.random.split(base, 2)
    entries = jnp.clip(jax.random.normal(key_off, (P_SIZE, P_SIZE), jnp.float32), -4.0, 4.0)
    off_part = (entries + entries.T) * (0.03 / math.sqrt(2.0))
    diag_part = jax.random.uniform(key_diag, (P_SIZE,), jnp.float32, 2.0, 6.0)
    on_diagonal = jnp.arange(P_SIZE)[:, None] == jnp.arange(P_SIZE)[None, :]
    return jnp.where(on_diagonal, diag_part[:, None] + 0.0 * off_part, off_part)


def steps_of(key, extent, pieces, least, largest):
    loudness, own = 1.0, jax.random.fold_in(key, 6)
    for dim, parts in pieces:
        steps = jnp.exp(jax.random.uniform(jax.random.fold_in(own, dim), (parts,), jnp.float32, least / len(pieces), largest / len(pieces)))
        loudness = loudness * jnp.repeat(steps, extent[dim] // parts).reshape([-1 if axis == dim else 1 for axis in range(len(extent))])
    return loudness


def length_profile(amount, total, most, slope):
    portions = [(1 << 20) // math.isqrt(standing ** slope) + 1 for standing in range(2, amount + 1)]
    surplus, counts = total - most - (amount - 1), [1] * (amount - 1)
    while surplus > 0:
        movable = [i for i in range(amount - 1) if counts[i] < most]
        whole, remaining = sum([portions[i] for i in movable]), surplus
        for i in movable:
            more = min(most - counts[i], max(1, remaining * portions[i] // whole), surplus)
            counts[i] = counts[i] + more
            surplus = surplus - more
    return np.array([most] + counts)


def uneven(own_key, amount, total, reach, lean):
    if amount == 2:
        one = jax.random.randint(own_key, (), max(1, total - reach), min(reach, total - 1) + 1)
        return jnp.stack([one, total - one])
    lengths = jnp.asarray(length_profile(amount, total, reach, lean), jnp.int32)
    twos = (amount - 1) // 2
    giver, receiver = lengths[1:1 + 2 * twos:2], lengths[2:2 + 2 * twos:2]
    slack = jnp.minimum(giver - 1, reach - receiver)
    moved = jax.random.randint(jax.random.fold_in(own_key, 1), (twos,), 0, 1 << 20) % (slack + 1)
    lengths = lengths.at[1:1 + 2 * twos:2].set(giver - moved).at[2:2 + 2 * twos:2].set(receiver + moved)
    return lengths[jax.random.permutation(jax.random.fold_in(own_key, 2), amount)]


def gaussian(rng, extent, width, limit, cuts=(), held_as=jnp.bfloat16):
    result = width * jax.random.normal(rng, extent, jnp.float32)
    if cuts:
        result = result * steps_of(rng, extent, cuts, -0.22, 0.18)
    return jnp.clip(result, -limit, limit).astype(held_as)


def setup_inputs(seed: int = 0) -> dict:
    splits = jax.random.split(jax.random.key(seed), 7)
    return {
        "design": gaussian(splits[0], (OBS, COEF), OBS ** -0.5, 0.25, ((0, 4), (1, 8))),
        "nuisance_vals": gaussian(splits[1], (NPA, OBS), (OBS // NARC) ** -0.5, 2.0, ((1, 4),), jnp.float32),
        "arc_index": jnp.searchsorted(jnp.cumsum(uneven(splits[2], NARC, OBS, 2 * OBS // NARC, 1)), jnp.arange(OBS), side="right").astype(jnp.int32),
        "filter_taps": gaussian(splits[3], (LAG,), LAG ** -0.5, 0.5, (), jnp.float32),
        "ordering": jax.random.permutation(splits[4], P_SIZE).astype(jnp.int32),
        "normal_prior": draw_normal_prior(jax.random.fold_in(splits[6], 71), 0),
    }


def nuisance_block(nuisance_vals, arc_index):
    columns = jnp.arange(NUIS)
    selector = ((columns % NPA)[None, :] == jnp.arange(NPA)[:, None]).astype(jnp.float32)
    picked = jnp.dot(nuisance_vals.T, selector, precision=lax.Precision.HIGHEST, preferred_element_type=jnp.float32)
    return jnp.where(arc_index[:, None] == (columns // NPA)[None, :], picked, jnp.float32(0.0))


def reference(design, nuisance_vals, arc_index, filter_taps, ordering, normal_prior):
    nuisance = nuisance_block(nuisance_vals, arc_index)
    raw = jnp.concatenate([design.astype(jnp.float32), nuisance], 1)
    padded = jnp.concatenate([jnp.zeros((LAG - 1, P_SIZE), jnp.float32), raw], 0)

    def add_lag(step, running):
        start = (LAG - 1 - step).astype(jnp.int32)
        window = lax.dynamic_slice(padded, (start, jnp.int32(0)), (OBS, P_SIZE))
        return running + filter_taps[step] * window

    filtered = lax.fori_loop(0, LAG, add_lag, jnp.zeros((OBS, P_SIZE), jnp.float32)).astype(jnp.bfloat16)
    inverse = jnp.argsort(ordering).astype(jnp.int32)
    ordered = filtered[:, inverse].astype(jnp.float32)
    update = lax.dot_general(ordered, ordered, (((0,), (0,)), ((), ())), preferred_element_type=jnp.float32)
    return normal_prior + update
```

```python
import functools
import math

import jax
import jax.numpy as jnp
from jax import lax
from jax.experimental import pallas as pl
from jax.experimental.pallas import tpu as pltpu
from jax.sharding import PartitionSpec as P

LANES = 128
MIB = 2**20
VM = pl.BlockSpec(memory_space=pltpu.VMEM)
SM = pl.BlockSpec(memory_space=pltpu.SMEM)
HB = pl.BlockSpec(memory_space=pltpu.HBM)
BF, F32, I32 = jnp.bfloat16, jnp.float32, jnp.int32


def capacity(width, groups):
    share = width / groups
    return -(-math.ceil(share + 3.9 * math.sqrt(share * (1 - 1 / groups))) // 16) * 16


def ring_order(count):
    depth = math.gcd(count, 4)
    side = count // depth
    order = [z * side for z in range(depth)]
    for turn, z in enumerate(reversed(range(depth))):
        ys = range(1, side) if turn % 2 == 0 else range(side - 1, 0, -1)
        order += [z * side + y for y in ys]
    return order


def swapped(x, axis, distance):
    return lax.ppermute(x, axis, [(i, i ^ distance) for i in range(lax.axis_size(axis))])


def toeplitz(taps, rows):
    period = 2 * rows + 1
    padded = jnp.concatenate([taps, jnp.zeros((period - taps.shape[0],), F32)])
    return jnp.tile(padded, rows)[: rows * 2 * rows].reshape(rows, 2 * rows)


def kernel_call(body, name, limit, flops, moved, **kw):
    return pl.pallas_call(
        body,
        name=name,
        compiler_params=pltpu.CompilerParams(vmem_limit_bytes=limit * MIB),
        cost_estimate=pl.CostEstimate(flops=flops, bytes_accessed=moved, transcendentals=0),
        **kw,
    )


def own_slots(order_ref, width):
    chunks = -(-width // LANES)
    total = order_ref.shape[0] * LANES
    begin = lax.axis_index("col") * width
    first, shift = begin // LANES, lax.rem(begin, LANES)
    rows = [order_ref[pl.ds(first + i, 1), :] for i in range(chunks + 1)]
    turn = lax.rem(LANES - shift, LANES)
    near = pltpu.roll(jnp.concatenate(rows[:-1], 0), turn, 1)
    far = pltpu.roll(jnp.concatenate(rows[1:], 0), turn, 1)
    lane = lax.broadcasted_iota(I32, (chunks, LANES), 1)
    index = lax.broadcasted_iota(I32, (chunks, LANES), 0) * LANES + lane
    slots = jnp.where(lane < LANES - shift, near, far)
    return jnp.where(index < width, slots, total)


def select_kernel(axis, share, cap, width, order_ref, raw_ref, *refs):
    outs, full = refs[:-1], refs[-1]
    slots = own_slots(order_ref, width)
    chunks = slots.shape[0]
    full[pl.ds(0, width), :] = raw_ref[...]
    if chunks * LANES > width:
        rest = chunks * LANES - width
        full[pl.ds(width, rest), :] = jnp.zeros((rest, full.shape[1]), BF)
    lane = lambda d: lax.broadcasted_iota(I32, (LANES, LANES), d)
    earlier = jnp.where(lane(0) < lane(1), 1.0, 0.0).astype(BF)
    chunk = lambda d: lax.broadcasted_iota(I32, (chunks, chunks), d)
    above = jnp.where(chunk(1) < chunk(0), 1.0, 0.0).astype(BF)
    buckets = len(outs) if len(outs) > 1 else outs[0].shape[0] // cap

    def bucket(which, store):
        low = which * share
        inside = (slots >= low) & (slots < low + share)
        marks = jnp.where(inside, 1.0, 0.0).astype(BF)
        within = jnp.dot(marks, earlier, preferred_element_type=F32)
        before = jnp.dot(above, marks, preferred_element_type=F32)
        rank = (within + jnp.sum(before, axis=1, keepdims=True)).astype(I32)
        rank = jnp.where(inside, rank, -1)
        row = lax.broadcasted_iota(I32, (cap, LANES), 0)
        hot = jnp.concatenate(
            [
                jnp.where(row == rank[q : q + 1, :], 1.0, 0.0).astype(BF)
                for q in range(chunks)
            ],
            1,
        )
        store(jnp.dot(hot, full[...], preferred_element_type=F32).astype(BF))

    if len(outs) > 1:
        me = lax.axis_index(axis)
        for m, out in enumerate(outs):

            def store(got, out=out):
                out[...] = got

            bucket(m ^ me, store)
    else:

        @pl.loop(0, buckets)
        def _(m):
            def store(got):
                outs[0][pl.ds(pl.multiple_of(m * cap, 16), cap), :] = got

            bucket(m, store)


def select(raw, order, axis, share, cap, buckets, split):
    width, times = raw.shape
    chunks = -(-width // LANES)
    if split:
        shape = [jax.ShapeDtypeStruct((cap, times), BF)] * buckets
    else:
        shape = [jax.ShapeDtypeStruct((buckets * cap, times), BF)]
    return kernel_call(
        functools.partial(select_kernel, axis, share, cap, width),
        "select",
        12,
        2 * buckets * cap * chunks * LANES * 256,
        2 * (width + buckets * cap) * times,
        out_shape=shape,
        in_specs=[VM, VM],
        out_specs=[VM] * len(shape),
        scratch_shapes=[pltpu.VMEM((chunks * LANES, times), BF)],
    )(order, raw)


def filter_rows(toep_ref, pieces, acc):
    me = lax.axis_index("row")
    times = toep_ref.shape[0]
    high = toep_ref[...].astype(BF)
    low = (toep_ref[...] - high.astype(F32)).astype(BF)
    rows = acc.shape[0]
    block = math.gcd(rows, 256)

    @pl.loop(0, rows // block)
    def _(i):
        there = pl.ds(pl.multiple_of(i * block, block), block)
        acc[there, :] = jnp.zeros((block, acc.shape[1]), F32)
        for m, piece in enumerate(pieces):
            x = piece[there, :]
            got = jnp.dot(x, high, preferred_element_type=F32)
            got = got + jnp.dot(x, low, preferred_element_type=F32)
            at = pl.ds(pl.multiple_of((m ^ me) * times, times), 2 * times)
            acc[there, at] = acc[there, at] + got


def filter_kernel(toep_ref, *refs):
    pieces, out, acc = refs[:-2], refs[-2], refs[-1]
    filter_rows(toep_ref, pieces, acc)
    out[...] = acc[:, : out.shape[1]].astype(BF)


def filtered(pieces, toep):
    rows, times = pieces[0].shape
    count = len(pieces)
    return kernel_call(
        filter_kernel,
        "filter",
        12 + rows * (count + 1) * times * 4 // MIB,
        8 * rows * count * times * times,
        4 * rows * count * times,
        out_shape=jax.ShapeDtypeStruct((rows, count * times), BF),
        in_specs=[VM] * (1 + count),
        out_specs=VM,
        scratch_shapes=[pltpu.VMEM((rows, (count + 1) * times), F32)],
    )(toep, *pieces)


def put_rows(list_ref, begin, rows, panel):
    @pl.loop(0, rows.shape[0] // 16)
    def _(g):
        at = pl.multiple_of(g * 16, 16)
        to = [list_ref[begin + at + q] for q in range(16)]
        values = rows[pl.ds(at, 16), :].astype(F32)
        for q in range(16):
            panel[pl.ds(to[q], 1), :] = values[q : q + 1, :]


def bring(copies):
    for copy in copies:
        copy.start()
    for copy in copies:
        copy.wait()


def ring_source(walk_ref, cols, step):
    return walk_ref[lax.axis_index("col") * cols + step]


def first_place_kernel(steps, cols, cap, rounds_ref, walk_ref, list_ref, extra_ref, *refs):
    nuis, old, prior = refs[:3]
    shards, (panel, kept, sem) = refs[3:-3], refs[-3:]
    fetch = pltpu.make_async_copy(prior, kept, sem.at[0])
    fetch.start()

    @pl.when(rounds_ref[0] > 1)
    def _():
        bring([pltpu.make_async_copy(old, panel, sem.at[1])])

    for step, shard in zip(steps, shards):
        put_rows(list_ref, ring_source(walk_ref, cols, step) * cap, shard, panel)
    put_rows(extra_ref, 0, nuis, panel)
    fetch.wait()


def first_place(shards, steps, rounds, walk, listed, extra, nuis, old, prior, cols, cap):
    return kernel_call(
        functools.partial(first_place_kernel, steps, cols, cap),
        "place",
        6,
        0,
        4 * prior.size,
        out_shape=[
            jax.ShapeDtypeStruct(old.shape, F32),
            jax.ShapeDtypeStruct(prior.shape, F32),
        ],
        in_specs=[SM, SM, SM, SM, VM, HB, HB] + [VM] * len(shards),
        out_specs=[VM, VM],
        scratch_shapes=[pltpu.SemaphoreType.DMA((2,))],
    )(rounds, walk, listed, extra, nuis, old, prior, *shards)


def place_kernel(steps, cols, cap, walk_ref, list_ref, *refs):
    shards, panel = refs[: len(steps)], refs[-1]
    for step, shard in zip(steps, shards):
        put_rows(list_ref, ring_source(walk_ref, cols, step) * cap, shard, panel)


def place(shards, steps, walk, listed, panel, cols, cap):
    return kernel_call(
        functools.partial(place_kernel, steps, cols, cap),
        "place",
        6,
        0,
        12 * sum(s.size for s in shards),
        out_shape=jax.ShapeDtypeStruct(panel.shape, F32),
        in_specs=[SM, SM] + [VM] * (len(shards) + 1),
        out_specs=VM,
        input_output_aliases={2 + len(shards): 0},
    )(walk, listed, *shards, panel)


def columns_kernel(count, cap, rounds_ref, list_ref, extra_ref, toep_ref, nuis, old, *refs):
    pieces, (out, acc, panel, sem) = refs[:count], refs[count:]
    span = panel.shape[1]

    @pl.when(rounds_ref[0] > 1)
    def _():
        bring([pltpu.make_async_copy(old, panel, sem)])

    filter_rows(toep_ref, pieces, acc)
    put_rows(list_ref, 0, acc.at[:, pl.ds(0, span)], panel)
    put_rows(extra_ref, 0, nuis, panel)
    wide = out.shape[1]
    for at in range(0, wide, LANES):
        size = min(LANES, wide - at)
        out[:, at : at + size] = panel[at : at + size, :].T.astype(BF)


def columns(pieces, rounds, listed, extra, nuis, toep, old, cap):
    rows, times = pieces[0].shape
    count = len(pieces)
    high, span = old.shape
    held = 4 * rows * (span + times) + 6 * high * span
    held += sum(2 * p.size for p in pieces[4:])
    return kernel_call(
        functools.partial(columns_kernel, count, cap),
        "columns",
        3 + held // MIB,
        8 * rows * span * times,
        12 * rows * span,
        out_shape=jax.ShapeDtypeStruct((span, high - 8), BF),
        in_specs=[SM, SM, SM, VM, VM, HB] + [VM] * count,
        out_specs=VM,
        scratch_shapes=[
            pltpu.VMEM((rows, span + times), F32),
            pltpu.VMEM((high, span), F32),
            pltpu.SemaphoreType.DMA,
        ],
    )(rounds, listed, extra, toep, nuis, old, *pieces)


def update_kernel(begins, step, cols, cap, block, walk_ref, list_ref, *refs):
    shards = refs[: len(begins)]
    weights, prior, _, out, panel, held, sems = refs[len(begins) :]
    source = ring_source(walk_ref, cols, step) * cap
    for begin, shard in zip(begins, shards):
        put_rows(list_ref, source + begin, shard, panel)
    steps, slots = prior.shape[0] // block, held.shape[0]

    def drain(i, slot):
        there = out.at[pl.ds(pl.multiple_of(i * block, 8), block), :]
        return pltpu.make_async_copy(held.at[slot], there, sems.at[slot])

    @pl.loop(0, steps)
    def _(i):
        slot = lax.rem(i, slots)

        @pl.when(i >= slots)
        def _():
            drain(i - slots, slot).wait()

        at = pl.ds(pl.multiple_of(i * block, 8), block)
        rows = panel[at, :].astype(BF)
        wide = prior.shape[1]
        for begin in range(0, wide, 2 * LANES):
            tile = pl.ds(begin, min(2 * LANES, wide - begin))
            got = jnp.dot(rows, weights[:, tile], preferred_element_type=F32)
            held[slot, :, tile] = prior[at, tile] + got
        drain(i, slot).start()

    for i in range(max(0, steps - slots), steps):
        drain(i, i % slots).wait()


def update(shards, begins, step, walk, listed, panel, weights, prior, cols, cap):
    high, wide = prior.shape
    span = weights.shape[0]
    block = max(b for b in range(16, 513, 16) if high % b == 0)
    slots = min(2, high // block)
    count = len(shards)
    return kernel_call(
        functools.partial(update_kernel, begins, step, cols, cap, block),
        "update",
        12,
        2 * high * wide * span,
        8 * high * wide,
        out_shape=[
            jax.ShapeDtypeStruct(prior.shape, F32),
            jax.ShapeDtypeStruct(panel.shape, F32),
        ],
        in_specs=[SM, SM] + [VM] * (count + 3),
        out_specs=[HB, VM],
        input_output_aliases={4 + count: 1},
        scratch_shapes=[
            pltpu.VMEM((slots, block, wide), F32),
            pltpu.SemaphoreType.DMA((slots,)),
        ],
    )(walk, listed, *shards, weights, prior, panel)[0]


def nuisance_kernel(every_ref, toep_ref, out, acc):
    groups, lines, times = every_ref.shape
    count, params = out.shape[0], lines - 1
    column = lax.broadcasted_iota(I32, (count, times), 0)
    owner = (column // params).astype(F32)
    acc[...] = jnp.zeros_like(acc)
    for s in range(groups):
        picked = jnp.zeros((count, times), F32)
        for q in range(params):
            picked = jnp.where(lax.rem(column, params) == q, every_ref[s, q : q + 1, :], picked)
        raw = jnp.where(every_ref[s, params:lines, :] == owner, picked, 0.0)
        got = jnp.dot(
            raw, toep_ref[...], precision=lax.Precision.HIGHEST, preferred_element_type=F32
        )
        at = slice(s * times, (s + 2) * times)
        acc[:, at] = acc[:, at] + got
    out[...] = acc[:, : out.shape[1]].astype(BF).astype(F32)


def filtered_nuisance(nuisance_vals, arc_index, toep, count):
    groups = lax.axis_size("row")
    params, times = nuisance_vals.shape
    own = jnp.concatenate([nuisance_vals, arc_index.astype(F32)[None]], 0)
    every = lax.all_to_all(
        jnp.broadcast_to(own[None], (groups,) + own.shape), "row", 0, 0, tiled=True
    )
    return kernel_call(
        nuisance_kernel,
        "nuisance",
        8,
        24 * groups * count * times * times,
        4 * count * groups * times,
        out_shape=jax.ShapeDtypeStruct((count, groups * times), F32),
        in_specs=[VM, VM],
        out_specs=VM,
        scratch_shapes=[pltpu.VMEM((count, (groups + 1) * times), F32)],
    )(every, toep)


def keys_kernel(bits, shares, caps, slots_ref, keys, rounds):
    slots = slots_ref[...]
    groups, width = slots.shape
    key = (lax.broadcasted_iota(I32, slots.shape, 1) << bits) | slots
    need = jnp.int32(1)
    for i, (axis, share, cap) in enumerate(zip(("row", "col"), shares, caps)):
        low = lax.axis_index(axis) * share
        inside = (slots >= low) & (slots < low + share)
        keys[i * groups : (i + 1) * groups, :] = jnp.where(inside, key, width << bits)
        most = jnp.zeros((groups, 1), F32)
        for b in range(lax.axis_size(axis)):
            mark = (slots >= b * share) & (slots < (b + 1) * share)
            found = jnp.sum(jnp.where(mark, 1.0, 0.0), axis=1, keepdims=True)
            most = jnp.maximum(most, found)
        need = jnp.maximum(need, (jnp.max(most).astype(I32) + cap - 1) // cap)
    rounds[0] = need


def overflow_round(step, raw, slots, ordering, toep, sizes, panels):
    (row_share, cap_row), (col_share, cap_col) = sizes
    times = raw.shape[1]
    rows, cols = lax.axis_size("row"), lax.axis_size("col")
    r, c = lax.axis_index("row"), lax.axis_index("col")
    own = slots[c]

    def buckets(share, cap, groups):
        owner = own // share
        hit = owner == jnp.arange(groups)[:, None]
        rank = jnp.sum(jnp.where(hit, jnp.cumsum(hit.astype(I32), axis=1), 0), axis=0) - 1
        rank = rank - step * cap
        to = jnp.where((rank >= 0) & (rank < cap), owner * cap + rank, -1)
        hot = (jnp.arange(groups * cap)[:, None] == to[None, :]).astype(BF)
        got = jnp.dot(hot, raw, preferred_element_type=F32).astype(BF)
        return got.reshape(groups, cap, times)

    def listing(share, cap, index):
        hit = slots // share == index
        rank = jnp.cumsum(hit.astype(I32), axis=1) - 1
        to = jnp.where(hit, rank - step * cap, -1)
        hot = to[:, None, :] == jnp.arange(cap)[None, :, None]
        code = jnp.where(hot, slots[:, None, :] - index * share + 1, 0)
        found = jnp.sum(code, axis=2)
        return jnp.where(found > 0, found - 1, share)

    def filter_all(x):
        return filtered([lax.dynamic_index_in_dim(x, m ^ r, 0, False) for m in range(rows)], toep)

    def everywhere(x, axis):
        size = lax.axis_size(axis)
        return lax.all_to_all(jnp.broadcast_to(x[None], (size,) + x.shape), axis, 0, 0, tiled=True)

    got = lax.all_to_all(buckets(row_share, cap_row, rows), "row", 0, 0, tiled=True)
    shards = everywhere(filter_all(got), "col")
    held = lax.all_to_all(buckets(col_share, cap_col, cols), "col", 0, 0, tiled=True)
    held = filter_all(everywhere(held.reshape(cols * cap_col, times), "row"))
    row_list = listing(row_share, cap_row, r).reshape(-1)
    col_list = listing(col_share, cap_col, c).reshape(-1)
    span = held.shape[1]
    return (
        panels[0].at[row_list].set(shards.reshape(-1, span).astype(F32)),
        panels[1].at[col_list].set(held.astype(F32)),
    )


def per_device(design, nuisance_vals, arc_index, filter_taps, ordering, normal_prior):
    times, width = design.shape
    rows, cols = lax.axis_size("row"), lax.axis_size("col")
    total = ordering.shape[0]
    row_share, col_share = total // rows, total // cols
    span = rows * times
    extras = total - width * cols
    cap_row, cap_col = capacity(width, rows), capacity(width, cols)

    raw = design.T
    order2d = ordering.reshape(total // LANES, LANES)
    to_rows = select(raw, order2d, "row", row_share, cap_row, rows, True)
    pieces = [to_rows[0]] + [swapped(to_rows[m], "row", m) for m in range(1, rows)]
    (to_cols,) = select(raw, order2d, "col", col_share, cap_col, cols, False)
    mine = lax.all_to_all(to_cols, "col", 0, 0, tiled=True)
    toep = toeplitz(filter_taps, times)
    *pieces, _ = lax.optimization_barrier((*pieces, to_cols))
    shard = filtered(pieces, toep)

    ordering, vals, arcs, _ = lax.optimization_barrier(
        (ordering, nuisance_vals, arc_index, shard)
    )
    slots = ordering[: width * cols].reshape(cols, width)
    bits = (total - 1).bit_length()
    keys, rounds = kernel_call(
        functools.partial(
            keys_kernel, bits, (row_share, col_share), (cap_row, cap_col)
        ),
        "keys",
        4,
        0,
        12 * width * cols,
        out_shape=[
            jax.ShapeDtypeStruct((2 * cols, width), I32),
            jax.ShapeDtypeStruct((1,), I32),
        ],
        in_specs=[VM],
        out_specs=[VM, SM],
    )(slots)
    keys = lax.sort(keys, dimension=1)
    low_row = (lax.axis_index("row") * row_share).astype(I32)
    low_col = (lax.axis_index("col") * col_share).astype(I32)

    def listing(part, low, share, cap):
        part = part[:, :cap]
        found = (part & ((1 << bits) - 1)) - low
        return jnp.where(part < (width << bits), found, share).reshape(-1)

    row_list = listing(keys[:cols], low_row, row_share, cap_row)
    col_list = listing(keys[cols:], low_col, col_share, cap_col)

    def extra_list(low, share):
        at = ordering[width * cols :] - low
        return jnp.where((at >= 0) & (at < share), at, share)

    nuis = filtered_nuisance(vals, arcs, toep, extras)

    shapes = [(row_share + 8, span), (col_share + 8, span)]
    empty = kernel_call(
        lambda *refs: None,
        "empty",
        1,
        0,
        0,
        out_shape=[jax.ShapeDtypeStruct(s, F32) for s in shapes],
        out_specs=[HB, HB],
    )()
    sizes = ((row_share, cap_row), (col_share, cap_col))

    def more(carry):
        return carry[0] < rounds[0]

    def again(carry):
        step, *panels = carry
        panels = overflow_round(step, raw, slots, ordering, toep, sizes, panels)
        return (step + 1, *panels)

    _, old_rows, old_cols = lax.while_loop(more, again, (jnp.int32(1), *empty))

    order = ring_order(cols)
    ahead = [(order[i], order[(i + 1) % cols]) for i in range(cols)]
    back = [(b, a) for a, b in ahead]
    walk = jnp.array(
        [order[(order.index(i) + j) % cols] for i in range(cols) for j in range(cols)], I32
    )

    parts = {0: mine}
    distance = rows // 2
    while distance:
        for m in list(parts):
            parts[m ^ distance] = swapped(parts[m], "row", distance)
        distance //= 2

    steps, half = cols // 2, cap_row // 2
    half -= half % 16
    up = down = shard
    panel, prior = first_place(
        [shard],
        [0],
        rounds,
        walk,
        row_list,
        extra_list(low_row, row_share),
        nuis,
        old_rows,
        normal_prior,
        cols,
        cap_row,
    )
    batch, at = [], []
    for i in range(1, steps):
        up = lax.ppermute(up, "col", ahead)
        down = lax.ppermute(down, "col", back)
        batch += [up, down]
        at += [(cols - i) % cols, i]
        if i == steps - 1 or len(batch) >= 2:
            panel = place(batch, at, walk, row_list, panel, cols, cap_row)
            batch, at = [], []
    up = lax.ppermute(up[:half], "col", ahead)
    down = lax.ppermute(down[half:], "col", back)
    weights = columns(
        [parts[m] for m in range(rows)],
        rounds,
        col_list,
        extra_list(low_col, col_share),
        nuis,
        toep,
        old_cols,
        cap_col,
    )
    return update(
        [up, down], (0, half), steps, walk, row_list, panel, weights, prior, cols, cap_row
    )


def solution(mesh):
    return jax.shard_map(
        per_device,
        mesh=mesh,
        in_specs=(P("row", "col"), P(None, "row"), P("row"), P(), P(), P("row", "col")),
        out_specs=P("row", "col"),
        check_vma=False,
    )
```

```python
import functools
import math

import jax
import jax.numpy as jnp
from jax import lax
from jax.experimental import pallas as pl
from jax.experimental.pallas import tpu as pltpu
from jax.sharding import PartitionSpec as P


LANES = 128
MIB = 2**20
VM = pl.BlockSpec(memory_space=pltpu.VMEM)
SM = pl.BlockSpec(memory_space=pltpu.SMEM)
HB = pl.BlockSpec(memory_space=pltpu.HBM)
BF, F32, I32 = jnp.bfloat16, jnp.float32, jnp.int32


def capacity(width, groups):
    share = width / groups
    return -(-math.ceil(share + 3.9 * math.sqrt(share * (1 - 1 / groups))) // 16) * 16


def ring_order(count):
    depth = math.gcd(count, 4)
    side = count // depth
    order = [z * side for z in range(depth)]
    for turn, z in enumerate(reversed(range(depth))):
        ys = range(1, side) if turn % 2 == 0 else range(side - 1, 0, -1)
        order += [z * side + y for y in ys]
    return order


def swapped(x, axis, distance):
    return lax.ppermute(x, axis, [(i, i ^ distance) for i in range(lax.axis_size(axis))])


def toeplitz(taps, rows):
    period = 2 * rows + 1
    padded = jnp.concatenate([taps, jnp.zeros((period - taps.shape[0],), F32)])
    return jnp.tile(padded, rows)[: rows * 2 * rows].reshape(rows, 2 * rows)


def kernel_call(body, limit, flops, moved, **kw):
    return pl.pallas_call(
        body,
        compiler_params=pltpu.CompilerParams(vmem_limit_bytes=limit * MIB),
        cost_estimate=pl.CostEstimate(flops=flops, bytes_accessed=moved, transcendentals=0),
        **kw,
    )


def own_slots(order_ref, width):
    chunks = -(-width // LANES)
    total = order_ref.shape[0] * LANES
    begin = lax.axis_index("col") * width
    first, shift = begin // LANES, lax.rem(begin, LANES)
    rows = [order_ref[pl.ds(first + i, 1), :] for i in range(chunks + 1)]
    turn = lax.rem(LANES - shift, LANES)
    near = pltpu.roll(jnp.concatenate(rows[:-1], 0), turn, 1)
    far = pltpu.roll(jnp.concatenate(rows[1:], 0), turn, 1)
    lane = lax.broadcasted_iota(I32, (chunks, LANES), 1)
    index = lax.broadcasted_iota(I32, (chunks, LANES), 0) * LANES + lane
    slots = jnp.where(lane < LANES - shift, near, far)
    return jnp.where(index < width, slots, total)


def select_kernel(axis, share, cap, width, order_ref, raw_ref, *refs):
    outs, full = refs[:-1], refs[-1]
    slots = own_slots(order_ref, width)
    chunks = slots.shape[0]
    full[pl.ds(0, width), :] = raw_ref[...]
    if chunks * LANES > width:
        rest = chunks * LANES - width
        full[pl.ds(width, rest), :] = jnp.zeros((rest, full.shape[1]), BF)
    lane = lambda d: lax.broadcasted_iota(I32, (LANES, LANES), d)
    earlier = jnp.where(lane(0) < lane(1), 1.0, 0.0).astype(BF)
    chunk = lambda d: lax.broadcasted_iota(I32, (chunks, chunks), d)
    above = jnp.where(chunk(1) < chunk(0), 1.0, 0.0).astype(BF)
    buckets = len(outs) if len(outs) > 1 else outs[0].shape[0] // cap

    def bucket(which, store):
        low = which * share
        inside = (slots >= low) & (slots < low + share)
        marks = jnp.where(inside, 1.0, 0.0).astype(BF)
        within = jnp.dot(marks, earlier, preferred_element_type=F32)
        before = jnp.dot(above, marks, preferred_element_type=F32)
        rank = (within + jnp.sum(before, axis=1, keepdims=True)).astype(I32)
        rank = jnp.where(inside, rank, -1)
        row = lax.broadcasted_iota(I32, (cap, LANES), 0)
        hot = jnp.concatenate(
            [
                jnp.where(row == rank[q : q + 1, :], 1.0, 0.0).astype(BF)
                for q in range(chunks)
            ],
            1,
        )
        store(jnp.dot(hot, full[...], preferred_element_type=F32).astype(BF))

    if len(outs) > 1:
        me = lax.axis_index(axis)
        for m, out in enumerate(outs):

            def store(got, out=out):
                out[...] = got

            bucket(m ^ me, store)
    else:

        @pl.loop(0, buckets)
        def _(m):
            def store(got):
                outs[0][pl.ds(pl.multiple_of(m * cap, 16), cap), :] = got

            bucket(m, store)


def select(raw, order, axis, share, cap, buckets, split):
    width, times = raw.shape
    chunks = -(-width // LANES)
    if split:
        shape = [jax.ShapeDtypeStruct((cap, times), BF)] * buckets
    else:
        shape = [jax.ShapeDtypeStruct((buckets * cap, times), BF)]
    return kernel_call(
        functools.partial(select_kernel, axis, share, cap, width),
        12,
        2 * buckets * cap * chunks * LANES * 256,
        2 * (width + buckets * cap) * times,
        out_shape=shape,
        in_specs=[VM, VM],
        out_specs=[VM] * len(shape),
        scratch_shapes=[pltpu.VMEM((chunks * LANES, times), BF)],
    )(order, raw)


def filter_rows(toep_ref, pieces, line, out, begin=0):
    me = lax.axis_index("row")
    times = toep_ref.shape[0]
    taps = jnp.concatenate([toep_ref[:, times:], toep_ref[:, :times]], 0)
    high = taps.astype(BF)
    both = jnp.concatenate([high, (taps - high.astype(F32)).astype(BF)], 1)
    rows, block = out.shape[0], line.shape[0]
    line[:, :times] = jnp.zeros((block, times), BF)

    @pl.loop(0, rows // block)
    def _(i):
        there = pl.ds(pl.multiple_of(i * block, block), block)
        source = pl.ds(pl.multiple_of(begin + i * block, math.gcd(begin, block)), block)
        for m, piece in enumerate(pieces):
            at = pl.ds(pl.multiple_of(((m ^ me) + 1) * times, times), times)
            line[:, at] = piece[source, :]
        for s in range(len(pieces)):
            got = jnp.dot(
                line[:, s * times : (s + 2) * times], both, preferred_element_type=F32
            )
            got = got[:, :times] + got[:, times:]
            out[there, s * times : (s + 1) * times] = got.astype(out.dtype)


def filter_kernel(toep_ref, *refs):
    pieces, out, line = refs[:-2], refs[-2], refs[-1]
    filter_rows(toep_ref, pieces, line, out)


def filtered(pieces, toep):
    rows, times = pieces[0].shape
    count = len(pieces)
    return kernel_call(
        filter_kernel,
        12,
        8 * rows * count * times * times,
        4 * rows * count * times,
        out_shape=jax.ShapeDtypeStruct((rows, count * times), BF),
        in_specs=[VM] * (1 + count),
        out_specs=VM,
        scratch_shapes=[pltpu.VMEM((math.gcd(rows, 256), (count + 1) * times), BF)],
    )(toep, *pieces)


def put_rows(list_ref, begin, rows, panel):
    group = math.gcd(rows.shape[0], 32)

    @pl.loop(0, rows.shape[0] // group)
    def _(g):
        at = pl.multiple_of(g * group, group)
        to = [list_ref[begin + at + q] for q in range(group)]
        values = rows[pl.ds(at, group), :].astype(F32)
        for q in range(group):
            panel[pl.ds(to[q], 1), :] = values[q : q + 1, :]


def bring(copy):
    copy.start()
    copy.wait()


def ring_source(walk_ref, cols, step):
    return walk_ref[lax.axis_index("col") * cols + step]


def first_place_kernel(steps, cols, cap, rounds_ref, walk_ref, list_ref, extra_ref, *refs):
    nuis, old, _, _ = refs[:4]
    shards, (panel, sem) = refs[4:-2], refs[-2:]

    @pl.when(rounds_ref[0] > 1)
    def _():
        bring(pltpu.make_async_copy(old, panel, sem))

    for step, shard in zip(steps, shards):
        put_rows(list_ref, ring_source(walk_ref, cols, step) * cap, shard, panel)
    put_rows(extra_ref, 0, nuis, panel)


def first_place(shards, steps, rounds, walk, listed, extra, nuis, old, after, cols, cap):
    return kernel_call(
        functools.partial(first_place_kernel, steps, cols, cap),
        6,
        0,
        12 * sum(s.size for s in shards),
        out_shape=jax.ShapeDtypeStruct(old.shape, F32),
        in_specs=[SM, SM, SM, SM, VM, HB, SM, SM] + [VM] * len(shards),
        out_specs=VM,
        scratch_shapes=[pltpu.SemaphoreType.DMA],
    )(rounds, walk, listed, extra, nuis, old, *after, *shards)


def place_kernel(steps, cols, cap, walk_ref, list_ref, *refs):
    shards, panel = refs[: len(steps)], refs[-1]
    for step, shard in zip(steps, shards):
        put_rows(list_ref, ring_source(walk_ref, cols, step) * cap, shard, panel)


def place(shards, steps, walk, listed, panel, cols, cap):
    return kernel_call(
        functools.partial(place_kernel, steps, cols, cap),
        6,
        0,
        12 * sum(s.size for s in shards),
        out_shape=jax.ShapeDtypeStruct(panel.shape, F32),
        in_specs=[SM, SM] + [VM] * (len(shards) + 1),
        out_specs=VM,
        input_output_aliases={2 + len(shards): 0},
    )(walk, listed, *shards, panel)


def halves_kernel(half, up, down, first, second):
    first[...] = up[pl.ds(0, half), :]
    second[...] = down[pl.ds(half, second.shape[0]), :]


def halves_of(up, down, half):
    rows, span = up.shape
    return kernel_call(
        functools.partial(halves_kernel, half),
        3,
        0,
        8 * up.size,
        out_shape=[
            jax.ShapeDtypeStruct((half, span), BF),
            jax.ShapeDtypeStruct((rows - half, span), BF),
        ],
        in_specs=[VM, VM],
        out_specs=[VM, VM],
    )(up, down)


def columns_kernel(part, parts, rounds_ref, list_ref, extra_ref, toep_ref, nuis, old, *refs):
    first, last = part == 0, part == parts - 1
    if last:
        pieces, (out, panel, acc, line, sem) = refs[:-5], refs[-5:]
    else:
        pieces, (panel, acc, line, sem) = refs[:-4], refs[-4:]
    rows = acc.shape[0]
    if first:

        @pl.when(rounds_ref[0] > 1)
        def _():
            bring(pltpu.make_async_copy(old, panel, sem))

    filter_rows(toep_ref, pieces, line, acc, part * rows)
    put_rows(list_ref, part * rows, acc, panel)
    if first:
        put_rows(extra_ref, 0, nuis, panel)
    if last:
        wide = out.shape[1]
        for at in range(0, wide, LANES):
            size = min(LANES, wide - at)
            out[:, at : at + size] = panel[at : at + size, :].T.astype(BF)


def columns(part, parts, pieces, rounds, listed, extra, nuis, toep, old):
    rows, times = pieces[0].shape
    rows //= parts
    count = len(pieces)
    high, span = old.shape
    last = part == parts - 1
    outs = [jax.ShapeDtypeStruct((span, high - 8), BF), jax.ShapeDtypeStruct((high, span), F32)]
    held = 4 * rows * span + sum(2 * p.size for p in pieces[4:])
    return kernel_call(
        functools.partial(columns_kernel, part, parts),
        4 + held // MIB,
        8 * rows * span * times,
        12 * rows * span,
        out_shape=outs if last else outs[1],
        in_specs=[SM, SM, SM, VM, VM, HB if part == 0 else VM] + [VM] * count,
        out_specs=[VM, VM] if last else VM,
        input_output_aliases={} if part == 0 else {5: 1 if last else 0},
        scratch_shapes=[
            pltpu.VMEM((rows, span), F32),
            pltpu.VMEM((math.gcd(rows, 256), span + times), BF),
            pltpu.SemaphoreType.DMA,
        ],
    )(rounds, listed, extra, toep, nuis, old, *pieces)


def update_kernel(begins, step, cols, cap, block, parts, walk_ref, list_ref, *refs):
    shards, refs = refs[: len(begins)], refs[len(begins) :]
    weights, priors, (_, out, panel, held, sems) = refs[0], refs[1 : 1 + parts], refs[1 + parts :]
    source = ring_source(walk_ref, cols, step) * cap
    for begin, shard in zip(begins, shards):
        put_rows(list_ref, source + begin, shard, panel)
    slots, wide = held.shape[0], held.shape[2]
    each = priors[0].shape[0] // block

    def drain(i, slot):
        there = out.at[pl.ds(pl.multiple_of(i * block, 8), block), :]
        return pltpu.make_async_copy(held.at[slot], there, sems.at[slot])

    for part, prior in enumerate(priors):

        @pl.loop(part * each, (part + 1) * each)
        def _(i, part=part, prior=prior):
            slot = lax.rem(i, slots)

            @pl.when(i >= slots)
            def _():
                drain(i - slots, slot).wait()

            rows = panel[pl.ds(pl.multiple_of(i * block, 8), block), :].astype(BF)
            at = pl.ds(pl.multiple_of((i - part * each) * block, 8), block)
            for begin in range(0, wide, 2 * LANES):
                tile = pl.ds(begin, min(2 * LANES, wide - begin))
                got = jnp.dot(rows, weights[:, tile], preferred_element_type=F32)
                held[slot, :, tile] = prior[at, tile] + got
            drain(i, slot).start()

    steps = each * parts
    for i in range(max(0, steps - slots), steps):
        drain(i, i % slots).wait()


def update(shards, begins, step, walk, listed, panel, weights, priors, cols, cap):
    part, wide = priors[0].shape
    parts, span = len(priors), weights.shape[0]
    high = part * parts
    block = max(b for b in range(16, 513, 16) if part % b == 0)
    slots = min(2, high // block)
    count = len(shards)
    return kernel_call(
        functools.partial(update_kernel, begins, step, cols, cap, block, parts),
        12,
        2 * high * wide * span,
        8 * high * wide,
        out_shape=[
            jax.ShapeDtypeStruct((high, wide), F32),
            jax.ShapeDtypeStruct(panel.shape, F32),
        ],
        in_specs=[SM, SM] + [VM] * (count + 2 + parts),
        out_specs=[HB, VM],
        input_output_aliases={3 + parts + count: 1},
        scratch_shapes=[
            pltpu.VMEM((slots, block, wide), F32),
            pltpu.SemaphoreType.DMA((slots,)),
        ],
    )(walk, listed, *shards, weights, *priors, panel)[0]


def nuisance_kernel(toep_ref, *refs):
    pieces, out, acc = refs[:-2], refs[-2], refs[-1]
    me = lax.axis_index("row")
    lines, times = pieces[0].shape
    count, params = out.shape[0], lines - 1
    column = lax.broadcasted_iota(I32, (count, times), 0)
    owner = (column // params).astype(F32)
    acc[...] = jnp.zeros_like(acc)
    for m, piece in enumerate(pieces):
        picked = jnp.zeros((count, times), F32)
        for q in range(params):
            picked = jnp.where(lax.rem(column, params) == q, piece[q : q + 1, :], picked)
        raw = jnp.where(piece[params:lines, :] == owner, picked, 0.0)
        got = jnp.dot(
            raw, toep_ref[...], precision=lax.Precision.HIGHEST, preferred_element_type=F32
        )
        at = pl.ds(pl.multiple_of((m ^ me) * times, times), 2 * times)
        acc[:, at] = acc[:, at] + got
    out[...] = acc[:, : out.shape[1]].astype(BF).astype(F32)


def filtered_nuisance(pieces, toep, count):
    groups = len(pieces)
    times = pieces[0].shape[1]
    return kernel_call(
        nuisance_kernel,
        8,
        24 * groups * count * times * times,
        4 * count * groups * times,
        out_shape=jax.ShapeDtypeStruct((count, groups * times), F32),
        in_specs=[VM] * (1 + groups),
        out_specs=VM,
        scratch_shapes=[pltpu.VMEM((count, (groups + 1) * times), F32)],
    )(toep, *pieces)


def keys_kernel(bits, shares, caps, slots_ref, keys, rounds):
    slots = slots_ref[...]
    groups, width = slots.shape
    key = (lax.broadcasted_iota(I32, slots.shape, 1) << bits) | slots
    need = jnp.int32(1)
    for i, (axis, share, cap) in enumerate(zip(("row", "col"), shares, caps)):
        low = lax.axis_index(axis) * share
        inside = (slots >= low) & (slots < low + share)
        keys[i * groups : (i + 1) * groups, :] = jnp.where(inside, key, width << bits)
        most = jnp.zeros((groups, 1), F32)
        for b in range(lax.axis_size(axis)):
            mark = (slots >= b * share) & (slots < (b + 1) * share)
            found = jnp.sum(jnp.where(mark, 1.0, 0.0), axis=1, keepdims=True)
            most = jnp.maximum(most, found)
        need = jnp.maximum(need, (jnp.max(most).astype(I32) + cap - 1) // cap)
    rounds[0] = need


def overflow_round(step, raw, slots, toep, sizes, panels):
    (row_share, cap_row), (col_share, cap_col) = sizes
    times = raw.shape[1]
    rows, cols = lax.axis_size("row"), lax.axis_size("col")
    r, c = lax.axis_index("row"), lax.axis_index("col")
    own = slots[c]

    def buckets(share, cap, groups):
        owner = own // share
        hit = owner == jnp.arange(groups)[:, None]
        rank = jnp.sum(jnp.where(hit, jnp.cumsum(hit.astype(I32), axis=1), 0), axis=0) - 1
        rank = rank - step * cap
        to = jnp.where((rank >= 0) & (rank < cap), owner * cap + rank, -1)
        hot = (jnp.arange(groups * cap)[:, None] == to[None, :]).astype(BF)
        got = jnp.dot(hot, raw, preferred_element_type=F32).astype(BF)
        return got.reshape(groups, cap, times)

    def listing(share, cap, index):
        hit = slots // share == index
        rank = jnp.cumsum(hit.astype(I32), axis=1) - 1
        to = jnp.where(hit, rank - step * cap, -1)
        hot = to[:, None, :] == jnp.arange(cap)[None, :, None]
        code = jnp.where(hot, slots[:, None, :] - index * share + 1, 0)
        found = jnp.sum(code, axis=2)
        return jnp.where(found > 0, found - 1, share)

    def filter_all(x):
        return filtered([lax.dynamic_index_in_dim(x, m ^ r, 0, False) for m in range(rows)], toep)

    def everywhere(x, axis):
        size = lax.axis_size(axis)
        return lax.all_to_all(jnp.broadcast_to(x[None], (size,) + x.shape), axis, 0, 0, tiled=True)

    got = lax.all_to_all(buckets(row_share, cap_row, rows), "row", 0, 0, tiled=True)
    shards = everywhere(filter_all(got), "col")
    held = lax.all_to_all(buckets(col_share, cap_col, cols), "col", 0, 0, tiled=True)
    held = filter_all(everywhere(held.reshape(cols * cap_col, times), "row"))
    row_list = listing(row_share, cap_row, r).reshape(-1)
    col_list = listing(col_share, cap_col, c).reshape(-1)
    span = held.shape[1]
    return (
        panels[0].at[row_list].set(shards.reshape(-1, span).astype(F32)),
        panels[1].at[col_list].set(held.astype(F32)),
    )


def per_device(design, nuisance_vals, arc_index, filter_taps, ordering, normal_prior):
    times, width = design.shape
    rows, cols = lax.axis_size("row"), lax.axis_size("col")
    total = ordering.shape[0]
    row_share, col_share = total // rows, total // cols
    span = rows * times
    extras = total - width * cols
    cap_row, cap_col = capacity(width, rows), capacity(width, cols)

    raw = design.T
    order2d = ordering.reshape(total // LANES, LANES)
    to_rows = select(raw, order2d, "row", row_share, cap_row, rows, True)
    pieces = [to_rows[0]] + [swapped(to_rows[m], "row", m) for m in range(1, rows)]
    params = jnp.concatenate([nuisance_vals, arc_index.astype(F32)[None]], 0)
    params, _ = lax.optimization_barrier((params, to_rows[-1]))
    params = [params] + [swapped(params, "row", m) for m in range(1, rows)]
    late, _ = lax.optimization_barrier((raw, to_rows[-1]))
    (to_cols,) = select(late, order2d, "col", col_share, cap_col, cols, False)
    toep = toeplitz(filter_taps, times)
    *pieces, _ = lax.optimization_barrier((*pieces, to_cols))
    shard = filtered(pieces, toep)
    to_cols, _ = lax.optimization_barrier((to_cols, shard))
    mine = lax.all_to_all(to_cols, "col", 0, 0, tiled=True)

    ordering, _ = lax.optimization_barrier((ordering, shard))
    slots = ordering[: width * cols].reshape(cols, width)
    bits = (total - 1).bit_length()
    keys, rounds = kernel_call(
        functools.partial(
            keys_kernel, bits, (row_share, col_share), (cap_row, cap_col)
        ),
        4,
        0,
        12 * width * cols,
        out_shape=[
            jax.ShapeDtypeStruct((2 * cols, width), I32),
            jax.ShapeDtypeStruct((1,), I32),
        ],
        in_specs=[VM],
        out_specs=[VM, SM],
    )(slots)
    order = ring_order(cols)
    ahead = [(order[i], order[(i + 1) % cols]) for i in range(cols)]
    back = [(b, a) for a, b in ahead]
    walk = jnp.array(
        [order[(order.index(i) + j) % cols] for i in range(cols) for j in range(cols)], I32
    )

    up = lax.ppermute(shard, "col", ahead)
    down = lax.ppermute(shard, "col", back)
    keys = lax.sort(keys, dimension=1)
    low_row = (lax.axis_index("row") * row_share).astype(I32)
    low_col = (lax.axis_index("col") * col_share).astype(I32)

    def listing(part, low, share, cap):
        part = part[:, :cap]
        found = (part & ((1 << bits) - 1)) - low
        return jnp.where(part < (width << bits), found, share).reshape(-1)

    row_list = listing(keys[:cols], low_row, row_share, cap_row)
    col_list = listing(keys[cols:], low_col, col_share, cap_col)

    def extra_list(low, share):
        at = ordering[width * cols :] - low
        return jnp.where((at >= 0) & (at < share), at, share)

    nuis = filtered_nuisance(params, toep, extras)

    shapes = [(row_share + 8, span), (col_share + 8, span)]
    empty = kernel_call(
        lambda *refs: None,
        1,
        0,
        0,
        out_shape=[jax.ShapeDtypeStruct(s, F32) for s in shapes],
        out_specs=[HB, HB],
    )()
    sizes = ((row_share, cap_row), (col_share, cap_col))

    def more(carry):
        return carry[0] < rounds[0]

    def again(carry):
        step, *panels = carry
        panels = overflow_round(step, raw, slots, toep, sizes, panels)
        return (step + 1, *panels)

    _, old_rows, old_cols = lax.while_loop(more, again, (jnp.int32(1), *empty))

    parts = {0: mine}
    distance = rows // 2
    while distance:
        for m in list(parts):
            parts[m ^ distance] = swapped(parts[m], "row", distance)
        distance //= 2

    steps, half = cols // 2, cap_row // 2
    half -= half % 16
    row_extra = extra_list(low_row, row_share)
    col_extra = extra_list(low_col, col_share)
    halves = [parts[m] for m in range(rows)]

    def column_part(part, panel):
        return columns(part, 2, halves, rounds, col_list, col_extra, nuis, toep, panel)

    panel = None
    batch, at = [], []
    for i in range(1, steps):
        if i > 1:
            up = lax.ppermute(up, "col", ahead)
            down = lax.ppermute(down, "col", back)
            if panel is None:
                panel = first_place(
                    [shard],
                    [0],
                    rounds,
                    walk,
                    row_list,
                    row_extra,
                    nuis,
                    old_rows,
                    (col_list, col_extra),
                    cols,
                    cap_row,
                )
            panel = place(batch, at, walk, row_list, panel, cols, cap_row)
            batch, at = [], []
        batch += [up, down]
        at += [(cols - i) % cols, i]
    col_panel = column_part(0, old_cols)
    up, down = halves_of(up, down, half)
    up = lax.ppermute(up, "col", ahead)
    down = lax.ppermute(down, "col", back)
    panel = place(batch, at, walk, row_list, panel, cols, cap_row)
    weights, _ = column_part(1, col_panel)
    return update(
        [up, down],
        (0, half),
        steps,
        walk,
        row_list,
        panel,
        weights,
        [normal_prior],
        cols,
        cap_row,
    )


def solution(mesh):
    return jax.shard_map(
        per_device,
        mesh=mesh,
        in_specs=(P("row", "col"), P(None, "row"), P("row"), P(), P(), P("row", "col")),
        out_specs=P("row", "col"),
        check_vma=False,
    )
```

```python
import functools
import math

import jax
import jax.numpy as jnp
from jax import lax
from jax.experimental import pallas as pl
from jax.experimental.pallas import tpu as pltpu
from jax.sharding import PartitionSpec as P


LANES = 128
MIB = 2**20
VM = pl.BlockSpec(memory_space=pltpu.VMEM)
SM = pl.BlockSpec(memory_space=pltpu.SMEM)
HB = pl.BlockSpec(memory_space=pltpu.HBM)
BF, F32, I32 = jnp.bfloat16, jnp.float32, jnp.int32


def capacity(width, groups):
    share = width / groups
    return -(-math.ceil(share + 3.9 * math.sqrt(share * (1 - 1 / groups))) // 16) * 16


def ring_order(count):
    depth = math.gcd(count, 4)
    side = count // depth
    order = [z * side for z in range(depth)]
    for turn, z in enumerate(reversed(range(depth))):
        ys = range(1, side) if turn % 2 == 0 else range(side - 1, 0, -1)
        order += [z * side + y for y in ys]
    return order


def row_block(rows, most=400):
    return max(b for b in range(16, most + 1, 16) if rows % b == 0)


def swapped(x, axis, distance):
    return lax.ppermute(x, axis, [(i, i ^ distance) for i in range(lax.axis_size(axis))])


def toeplitz(taps, rows):
    period = 2 * rows + 1
    padded = jnp.concatenate([taps, jnp.zeros((period - taps.shape[0],), F32)])
    return jnp.tile(padded, rows)[: rows * 2 * rows].reshape(rows, 2 * rows)


def kernel_call(body, limit, flops, moved, **kw):
    return pl.pallas_call(
        body,
        compiler_params=pltpu.CompilerParams(vmem_limit_bytes=limit * MIB),
        cost_estimate=pl.CostEstimate(flops=flops, bytes_accessed=moved, transcendentals=0),
        **kw,
    )


def own_slots(order_ref, width):
    chunks = -(-width // LANES)
    total = order_ref.shape[0] * LANES
    begin = lax.axis_index("col") * width
    first, shift = begin // LANES, lax.rem(begin, LANES)
    rows = [order_ref[pl.ds(first + i, 1), :] for i in range(chunks + 1)]
    turn = lax.rem(LANES - shift, LANES)
    near = pltpu.roll(jnp.concatenate(rows[:-1], 0), turn, 1)
    far = pltpu.roll(jnp.concatenate(rows[1:], 0), turn, 1)
    lane = lax.broadcasted_iota(I32, (chunks, LANES), 1)
    index = lax.broadcasted_iota(I32, (chunks, LANES), 0) * LANES + lane
    slots = jnp.where(lane < LANES - shift, near, far)
    return jnp.where(index < width, slots, total)


def select_kernel(axis, share, cap, width, order_ref, raw_ref, *refs):
    outs, full = refs[:-1], refs[-1]
    slots = own_slots(order_ref, width)
    chunks = slots.shape[0]
    full[pl.ds(0, width), :] = raw_ref[...]
    if chunks * LANES > width:
        rest = chunks * LANES - width
        full[pl.ds(width, rest), :] = jnp.zeros((rest, full.shape[1]), BF)
    lane = lambda d: lax.broadcasted_iota(I32, (LANES, LANES), d)
    earlier = jnp.where(lane(0) < lane(1), 1.0, 0.0).astype(BF)
    chunk = lambda d: lax.broadcasted_iota(I32, (chunks, chunks), d)
    above = jnp.where(chunk(1) < chunk(0), 1.0, 0.0).astype(BF)
    buckets = len(outs) if len(outs) > 1 else outs[0].shape[0] // cap

    def bucket(which, store):
        low = which * share
        inside = (slots >= low) & (slots < low + share)
        marks = jnp.where(inside, 1.0, 0.0).astype(BF)
        within = jnp.dot(marks, earlier, preferred_element_type=F32)
        before = jnp.dot(above, marks, preferred_element_type=F32)
        rank = (within + jnp.sum(before, axis=1, keepdims=True)).astype(I32)
        rank = jnp.where(inside, rank, -1)
        row = lax.broadcasted_iota(I32, (cap, LANES), 0)
        hot = jnp.concatenate(
            [
                jnp.where(row == rank[q : q + 1, :], 1.0, 0.0).astype(BF)
                for q in range(chunks)
            ],
            1,
        )
        store(jnp.dot(hot, full[...], preferred_element_type=F32).astype(BF))

    if len(outs) > 1:
        me = lax.axis_index(axis)
        for m, out in enumerate(outs):

            def store(got, out=out):
                out[...] = got

            bucket(m ^ me, store)
    else:

        @pl.loop(0, buckets)
        def _(m):
            def store(got):
                outs[0][pl.ds(pl.multiple_of(m * cap, 16), cap), :] = got

            bucket(m, store)


def select(raw, order, axis, share, cap, buckets, split):
    width, times = raw.shape
    chunks = -(-width // LANES)
    if split:
        shape = [jax.ShapeDtypeStruct((cap, times), BF)] * buckets
    else:
        shape = [jax.ShapeDtypeStruct((buckets * cap, times), BF)]
    return kernel_call(
        functools.partial(select_kernel, axis, share, cap, width),
        12,
        2 * buckets * cap * chunks * LANES * 256,
        2 * (width + buckets * cap) * times,
        out_shape=shape,
        in_specs=[VM, VM],
        out_specs=[VM] * len(shape),
        scratch_shapes=[pltpu.VMEM((chunks * LANES, times), BF)],
    )(order, raw)


def filter_rows(toep_ref, pieces, line, out):
    me = lax.axis_index("row")
    times = toep_ref.shape[0]
    taps = jnp.concatenate([toep_ref[:, times:], toep_ref[:, :times]], 0)
    high = taps.astype(BF)
    both = jnp.concatenate([high, (taps - high.astype(F32)).astype(BF)], 1)
    rows, block = out.shape[0], line.shape[0]
    line[:, :times] = jnp.zeros((block, times), BF)

    @pl.loop(0, rows // block)
    def _(i):
        there = pl.ds(pl.multiple_of(i * block, block), block)
        for m, piece in enumerate(pieces):
            at = pl.ds(pl.multiple_of(((m ^ me) + 1) * times, times), times)
            line[:, at] = piece[there, :]
        for s in range(len(pieces)):
            got = jnp.dot(
                line[:, s * times : (s + 2) * times], both, preferred_element_type=F32
            )
            got = got[:, :times] + got[:, times:]
            out[there, s * times : (s + 1) * times] = got.astype(out.dtype)


def filter_kernel(toep_ref, *refs):
    pieces, out, line = refs[:-2], refs[-2], refs[-1]
    filter_rows(toep_ref, pieces, line, out)


def filtered(pieces, toep):
    rows, times = pieces[0].shape
    count = len(pieces)
    return kernel_call(
        filter_kernel,
        12,
        8 * rows * count * times * times,
        4 * rows * count * times,
        out_shape=jax.ShapeDtypeStruct((rows, count * times), BF),
        in_specs=[VM] * (1 + count),
        out_specs=VM,
        scratch_shapes=[pltpu.VMEM((row_block(rows), (count + 1) * times), BF)],
    )(toep, *pieces)


def put_rows(list_ref, begin, rows, panel, cap=None):
    group = math.gcd(rows.shape[0], 32 if cap is None else math.gcd(cap, 32))

    @pl.loop(0, rows.shape[0] // group)
    def _(g):
        at = pl.multiple_of(g * group, group)

        def put():
            to = [list_ref[begin + at + q] for q in range(group)]
            values = rows[pl.ds(at, group), :].astype(F32)
            for q in range(group):
                panel[pl.ds(to[q], 1), :] = values[q : q + 1, :]

        if cap is None:
            put()
        else:
            pl.when(list_ref[begin + at] < panel.shape[0] - 8)(put)


def bring(copy):
    copy.start()
    copy.wait()


def ring_source(walk_ref, cols, step):
    return walk_ref[lax.axis_index("col") * cols + step]


def first_place_kernel(steps, cols, cap, rounds_ref, walk_ref, list_ref, extra_ref, *refs):
    nuis, old, _, _ = refs[:4]
    shards, (panel, sem) = refs[4:-2], refs[-2:]

    @pl.when(rounds_ref[0] > 1)
    def _():
        bring(pltpu.make_async_copy(old, panel, sem))

    for step, shard in zip(steps, shards):
        put_rows(list_ref, ring_source(walk_ref, cols, step) * cap, shard, panel, cap)
    put_rows(extra_ref, 0, nuis, panel)


def first_place(shards, steps, rounds, walk, listed, extra, nuis, old, after, cols, cap):
    return kernel_call(
        functools.partial(first_place_kernel, steps, cols, cap),
        6,
        0,
        12 * sum(s.size for s in shards),
        out_shape=jax.ShapeDtypeStruct(old.shape, F32),
        in_specs=[SM, SM, SM, SM, VM, HB, SM, SM] + [VM] * len(shards),
        out_specs=VM,
        scratch_shapes=[pltpu.SemaphoreType.DMA],
    )(rounds, walk, listed, extra, nuis, old, *after, *shards)


def place_kernel(steps, cols, cap, walk_ref, list_ref, *refs):
    shards, panel = refs[: len(steps)], refs[-1]
    for step, shard in zip(steps, shards):
        put_rows(list_ref, ring_source(walk_ref, cols, step) * cap, shard, panel, cap)


def place(shards, steps, walk, listed, panel, cols, cap):
    return kernel_call(
        functools.partial(place_kernel, steps, cols, cap),
        6,
        0,
        12 * sum(s.size for s in shards),
        out_shape=jax.ShapeDtypeStruct(panel.shape, F32),
        in_specs=[SM, SM] + [VM] * (len(shards) + 1),
        out_specs=VM,
        input_output_aliases={2 + len(shards): 0},
    )(walk, listed, *shards, panel)


def halves_kernel(half, up, down, first, second):
    first[...] = up[pl.ds(0, half), :]
    second[...] = down[pl.ds(half, second.shape[0]), :]


def halves_of(up, down, half):
    rows, span = up.shape
    return kernel_call(
        functools.partial(halves_kernel, half),
        3,
        0,
        8 * up.size,
        out_shape=[
            jax.ShapeDtypeStruct((half, span), BF),
            jax.ShapeDtypeStruct((rows - half, span), BF),
        ],
        in_specs=[VM, VM],
        out_specs=[VM, VM],
    )(up, down)


def columns_kernel(part, parts, cap, rounds_ref, list_ref, extra_ref, toep_ref, nuis, old, *refs):
    first, last = part == 0, part == parts - 1
    if last:
        pieces, (out, panel, acc, line, sem) = refs[:-5], refs[-5:]
    else:
        pieces, (panel, acc, line, sem) = refs[:-4], refs[-4:]
    rows = acc.shape[0]
    if first:

        @pl.when(rounds_ref[0] > 1)
        def _():
            bring(pltpu.make_async_copy(old, panel, sem))

    filter_rows(toep_ref, pieces, line, acc)
    put_rows(list_ref, part * rows, acc, panel, cap)
    if first:
        put_rows(extra_ref, 0, nuis, panel)
    if last:
        wide = out.shape[1]
        for at in range(0, wide, LANES):
            size = min(LANES, wide - at)
            out[:, at : at + size] = panel[at : at + size, :].T.astype(BF)


def columns(part, parts, cap, pieces, rounds, listed, extra, nuis, toep, old):
    rows, times = pieces[0].shape
    count = len(pieces)
    high, span = old.shape
    last = part == parts - 1
    outs = [jax.ShapeDtypeStruct((span, high - 8), BF), jax.ShapeDtypeStruct((high, span), F32)]
    held = 4 * rows * span + sum(2 * p.size for p in pieces[4:])
    return kernel_call(
        functools.partial(columns_kernel, part, parts, cap),
        4 + held // MIB,
        8 * rows * span * times,
        12 * rows * span,
        out_shape=outs if last else outs[1],
        in_specs=[SM, SM, SM, VM, VM, HB if part == 0 else VM] + [VM] * count,
        out_specs=[VM, VM] if last else VM,
        input_output_aliases={} if part == 0 else {5: 1 if last else 0},
        scratch_shapes=[
            pltpu.VMEM((rows, span), F32),
            pltpu.VMEM((row_block(rows), span + times), BF),
            pltpu.SemaphoreType.DMA,
        ],
    )(rounds, listed, extra, toep, nuis, old, *pieces)


def update_kernel(begins, step, cols, cap, block, parts, walk_ref, list_ref, *refs):
    shards, refs = refs[: len(begins)], refs[len(begins) :]
    weights, priors, (_, out, panel, held, sems) = refs[0], refs[1 : 1 + parts], refs[1 + parts :]
    source = ring_source(walk_ref, cols, step) * cap
    for begin, shard in zip(begins, shards):
        put_rows(list_ref, source + begin, shard, panel, math.gcd(cap, shard.shape[0]))
    slots, wide = held.shape[0], held.shape[2]
    each = priors[0].shape[0] // block

    def drain(i, slot):
        there = out.at[pl.ds(pl.multiple_of(i * block, 8), block), :]
        return pltpu.make_async_copy(held.at[slot], there, sems.at[slot])

    for part, prior in enumerate(priors):

        @pl.loop(part * each, (part + 1) * each)
        def _(i, part=part, prior=prior):
            slot = lax.rem(i, slots)

            @pl.when(i >= slots)
            def _():
                drain(i - slots, slot).wait()

            rows = panel[pl.ds(pl.multiple_of(i * block, 8), block), :].astype(BF)
            at = pl.ds(pl.multiple_of((i - part * each) * block, 8), block)
            for begin in range(0, wide, 2 * LANES):
                tile = pl.ds(begin, min(2 * LANES, wide - begin))
                got = jnp.dot(rows, weights[:, tile], preferred_element_type=F32)
                held[slot, :, tile] = prior[at, tile] + got
            drain(i, slot).start()

    steps = each * parts
    for i in range(max(0, steps - slots), steps):
        drain(i, i % slots).wait()


def update(shards, begins, step, walk, listed, panel, weights, priors, cols, cap):
    part, wide = priors[0].shape
    parts, span = len(priors), weights.shape[0]
    high = part * parts
    block = max(b for b in range(16, 257, 16) if part % b == 0)
    slots = min(3, high // block)
    count = len(shards)
    return kernel_call(
        functools.partial(update_kernel, begins, step, cols, cap, block, parts),
        12,
        2 * high * wide * span,
        8 * high * wide,
        out_shape=[
            jax.ShapeDtypeStruct((high, wide), F32),
            jax.ShapeDtypeStruct(panel.shape, F32),
        ],
        in_specs=[SM, SM] + [VM] * (count + 2 + parts),
        out_specs=[HB, VM],
        input_output_aliases={3 + parts + count: 1},
        scratch_shapes=[
            pltpu.VMEM((slots, block, wide), F32),
            pltpu.SemaphoreType.DMA((slots,)),
        ],
    )(walk, listed, *shards, weights, *priors, panel)[0]


def nuisance_kernel(toep_ref, *refs):
    pieces, out, acc = refs[:-2], refs[-2], refs[-1]
    me = lax.axis_index("row")
    lines, times = pieces[0].shape
    count, params = out.shape[0], lines - 1
    column = lax.broadcasted_iota(I32, (count, times), 0)
    owner = (column // params).astype(F32)
    acc[...] = jnp.zeros_like(acc)
    for m, piece in enumerate(pieces):
        picked = jnp.zeros((count, times), F32)
        for q in range(params):
            picked = jnp.where(lax.rem(column, params) == q, piece[q : q + 1, :], picked)
        raw = jnp.where(piece[params:lines, :] == owner, picked, 0.0)
        got = jnp.dot(
            raw, toep_ref[...], precision=lax.Precision.HIGHEST, preferred_element_type=F32
        )
        at = pl.ds(pl.multiple_of((m ^ me) * times, times), 2 * times)
        acc[:, at] = acc[:, at] + got
    out[...] = acc[:, : out.shape[1]].astype(BF).astype(F32)


def filtered_nuisance(pieces, toep, count):
    groups = len(pieces)
    times = pieces[0].shape[1]
    return kernel_call(
        nuisance_kernel,
        8,
        24 * groups * count * times * times,
        4 * count * groups * times,
        out_shape=jax.ShapeDtypeStruct((count, groups * times), F32),
        in_specs=[VM] * (1 + groups),
        out_specs=VM,
        scratch_shapes=[pltpu.VMEM((count, (groups + 1) * times), F32)],
    )(toep, *pieces)


def keys_kernel(bits, shares, caps, slots_ref, keys, rounds):
    slots = slots_ref[...]
    groups, width = slots.shape
    key = (lax.broadcasted_iota(I32, slots.shape, 1) << bits) | slots
    need = jnp.int32(1)
    for i, (axis, share, cap) in enumerate(zip(("row", "col"), shares, caps)):
        low = lax.axis_index(axis) * share
        inside = (slots >= low) & (slots < low + share)
        keys[i * groups : (i + 1) * groups, :] = jnp.where(inside, key, width << bits)
        most = jnp.zeros((groups, 1), F32)
        for b in range(lax.axis_size(axis)):
            mark = (slots >= b * share) & (slots < (b + 1) * share)
            found = jnp.sum(jnp.where(mark, 1.0, 0.0), axis=1, keepdims=True)
            most = jnp.maximum(most, found)
        need = jnp.maximum(need, (jnp.max(most).astype(I32) + cap - 1) // cap)
    rounds[0] = need


def overflow_round(step, raw, slots, toep, sizes, panels):
    (row_share, cap_row), (col_share, cap_col) = sizes
    times = raw.shape[1]
    rows, cols = lax.axis_size("row"), lax.axis_size("col")
    r, c = lax.axis_index("row"), lax.axis_index("col")
    own = slots[c]

    def buckets(share, cap, groups):
        owner = own // share
        hit = owner == jnp.arange(groups)[:, None]
        rank = jnp.sum(jnp.where(hit, jnp.cumsum(hit.astype(I32), axis=1), 0), axis=0) - 1
        rank = rank - step * cap
        to = jnp.where((rank >= 0) & (rank < cap), owner * cap + rank, -1)
        hot = (jnp.arange(groups * cap)[:, None] == to[None, :]).astype(BF)
        got = jnp.dot(hot, raw, preferred_element_type=F32).astype(BF)
        return got.reshape(groups, cap, times)

    def listing(share, cap, index):
        hit = slots // share == index
        rank = jnp.cumsum(hit.astype(I32), axis=1) - 1
        to = jnp.where(hit, rank - step * cap, -1)
        hot = to[:, None, :] == jnp.arange(cap)[None, :, None]
        code = jnp.where(hot, slots[:, None, :] - index * share + 1, 0)
        found = jnp.sum(code, axis=2)
        return jnp.where(found > 0, found - 1, share)

    def filter_all(x):
        return filtered([lax.dynamic_index_in_dim(x, m ^ r, 0, False) for m in range(rows)], toep)

    def everywhere(x, axis):
        size = lax.axis_size(axis)
        return lax.all_to_all(jnp.broadcast_to(x[None], (size,) + x.shape), axis, 0, 0, tiled=True)

    got = lax.all_to_all(buckets(row_share, cap_row, rows), "row", 0, 0, tiled=True)
    shards = everywhere(filter_all(got), "col")
    held = lax.all_to_all(buckets(col_share, cap_col, cols), "col", 0, 0, tiled=True)
    held = filter_all(everywhere(held.reshape(cols * cap_col, times), "row"))
    row_list = listing(row_share, cap_row, r).reshape(-1)
    col_list = listing(col_share, cap_col, c).reshape(-1)
    span = held.shape[1]
    return (
        panels[0].at[row_list].set(shards.reshape(-1, span).astype(F32)),
        panels[1].at[col_list].set(held.astype(F32)),
    )


def per_device(design, nuisance_vals, arc_index, filter_taps, ordering, normal_prior):
    times, width = design.shape
    rows, cols = lax.axis_size("row"), lax.axis_size("col")
    total = ordering.shape[0]
    row_share, col_share = total // rows, total // cols
    span = rows * times
    extras = total - width * cols
    cap_row, cap_col = capacity(width, rows), capacity(width, cols)

    raw = design.T
    order2d = ordering.reshape(total // LANES, LANES)
    to_rows = select(raw, order2d, "row", row_share, cap_row, rows, True)
    pieces = [to_rows[0]] + [swapped(to_rows[m], "row", m) for m in range(1, rows)]
    late, _ = lax.optimization_barrier((raw, to_rows[-1]))
    (to_cols,) = select(late, order2d, "col", col_share, cap_col, cols, False)
    toep = toeplitz(filter_taps, times)
    *pieces, _ = lax.optimization_barrier((*pieces, to_cols))
    shard = filtered(pieces, toep)
    to_cols, _ = lax.optimization_barrier((to_cols, shard))
    mine = lax.all_to_all(to_cols, "col", 0, 0, tiled=True)

    params = jnp.concatenate([nuisance_vals, arc_index.astype(F32)[None]], 0)
    params, _ = lax.optimization_barrier((params, shard))
    params = [params] + [swapped(params, "row", m) for m in range(1, rows)]
    ordering, _ = lax.optimization_barrier((ordering, shard))
    slots = ordering[: width * cols].reshape(cols, width)
    bits = (total - 1).bit_length()
    keys, rounds = kernel_call(
        functools.partial(
            keys_kernel, bits, (row_share, col_share), (cap_row, cap_col)
        ),
        4,
        0,
        12 * width * cols,
        out_shape=[
            jax.ShapeDtypeStruct((2 * cols, width), I32),
            jax.ShapeDtypeStruct((1,), I32),
        ],
        in_specs=[VM],
        out_specs=[VM, SM],
    )(slots)
    order = ring_order(cols)
    ahead = [(order[i], order[(i + 1) % cols]) for i in range(cols)]
    back = [(b, a) for a, b in ahead]
    walk = jnp.array(
        [order[(order.index(i) + j) % cols] for i in range(cols) for j in range(cols)], I32
    )

    up = lax.ppermute(shard, "col", ahead)
    down = lax.ppermute(shard, "col", back)
    keys = lax.sort(keys, dimension=1)
    low_row = (lax.axis_index("row") * row_share).astype(I32)
    low_col = (lax.axis_index("col") * col_share).astype(I32)

    def listing(part, low, share, cap):
        part = part[:, :cap]
        found = (part & ((1 << bits) - 1)) - low
        return jnp.where(part < (width << bits), found, share).reshape(-1)

    row_list = listing(keys[:cols], low_row, row_share, cap_row)
    col_list = listing(keys[cols:], low_col, col_share, cap_col)

    def extra_list(low, share):
        at = ordering[width * cols :] - low
        return jnp.where((at >= 0) & (at < share), at, share)

    nuis = filtered_nuisance(params, toep, extras)

    shapes = [(row_share + 8, span), (col_share + 8, span)]
    empty = kernel_call(
        lambda *refs: None,
        1,
        0,
        0,
        out_shape=[jax.ShapeDtypeStruct(s, F32) for s in shapes],
        out_specs=[HB, HB],
    )()
    sizes = ((row_share, cap_row), (col_share, cap_col))

    def more(carry):
        return carry[0] < rounds[0]

    def again(carry):
        step, *panels = carry
        panels = overflow_round(step, raw, slots, toep, sizes, panels)
        return (step + 1, *panels)

    _, old_rows, old_cols = lax.while_loop(more, again, (jnp.int32(1), *empty))

    split = [{0: piece} for piece in halves_of(mine, mine, mine.shape[0] // 2)]
    distance = rows // 2
    while distance:
        for m in list(split[0]):
            for parts in split:
                parts[m ^ distance] = swapped(parts[m], "row", distance)
        distance //= 2

    steps, half = cols // 2, cap_row // 2
    half -= half % 16
    row_extra = extra_list(low_row, row_share)
    col_extra = extra_list(low_col, col_share)

    def column_part(part, panel):
        pieces = [split[part][m] for m in range(rows)]
        return columns(
            part, 2, cap_col, pieces, rounds, col_list, col_extra, nuis, toep, panel
        )

    panel = None
    batch, at = [], []
    for i in range(1, steps):
        if i > 1:
            up = lax.ppermute(up, "col", ahead)
            down = lax.ppermute(down, "col", back)
            if panel is None:
                panel = first_place(
                    [shard],
                    [0],
                    rounds,
                    walk,
                    row_list,
                    row_extra,
                    nuis,
                    old_rows,
                    (col_list, col_extra),
                    cols,
                    cap_row,
                )
            else:
                panel = place(batch, at, walk, row_list, panel, cols, cap_row)
                batch, at = [], []
        batch += [up, down]
        at += [(cols - i) % cols, i]
    col_panel = column_part(0, old_cols)
    up, down = halves_of(up, down, half)
    up = lax.ppermute(up, "col", ahead)
    down = lax.ppermute(down, "col", back)
    panel = place(batch, at, walk, row_list, panel, cols, cap_row)
    weights, _ = column_part(1, col_panel)
    return update(
        [up, down],
        (0, half),
        steps,
        walk,
        row_list,
        panel,
        weights,
        [normal_prior],
        cols,
        cap_row,
    )


def solution(mesh):
    return jax.shard_map(
        per_device,
        mesh=mesh,
        in_specs=(P("row", "col"), P(None, "row"), P("row"), P(), P(), P("row", "col")),
        out_specs=P("row", "col"),
        check_vma=False,
    )
```

```python
import functools
import math

import jax
import jax.numpy as jnp
from jax import lax
from jax.experimental import pallas as pl
from jax.experimental.pallas import tpu as pltpu
from jax.sharding import PartitionSpec as P


LANES = 128
MIB = 2**20
VM = pl.BlockSpec(memory_space=pltpu.VMEM)
SM = pl.BlockSpec(memory_space=pltpu.SMEM)
HB = pl.BlockSpec(memory_space=pltpu.HBM)
BF, F32, I32 = jnp.bfloat16, jnp.float32, jnp.int32


def capacity(width, groups):
    share = width / groups
    return -(-math.ceil(share + 3.9 * math.sqrt(share * (1 - 1 / groups))) // 16) * 16


def ring_order(count):
    depth = math.gcd(count, 4)
    side = count // depth
    order = [z * side for z in range(depth)]
    for turn, z in enumerate(reversed(range(depth))):
        ys = range(1, side) if turn % 2 == 0 else range(side - 1, 0, -1)
        order += [z * side + y for y in ys]
    return order


def row_block(rows, most=400):
    return max(b for b in range(16, most + 1, 16) if rows % b == 0)


def swapped(x, axis, distance):
    return lax.ppermute(x, axis, [(i, i ^ distance) for i in range(lax.axis_size(axis))])


def toeplitz(taps_ref, times):
    taps = taps_ref[...]
    rest = jnp.zeros((1, 2 * times - taps.shape[1]), F32)
    line = jnp.broadcast_to(jnp.concatenate([taps, rest], 1), (times, 2 * times))
    return pltpu.roll(line, 0, 1, stride=1, stride_axis=0)


def kernel_call(body, limit, flops, moved, **kw):
    return pl.pallas_call(
        body,
        compiler_params=pltpu.CompilerParams(vmem_limit_bytes=limit * MIB),
        cost_estimate=pl.CostEstimate(flops=flops, bytes_accessed=moved, transcendentals=0),
        **kw,
    )


def own_slots(order_ref, width):
    chunks = -(-width // LANES)
    total = order_ref.shape[0] * LANES
    begin = lax.axis_index("col") * width
    first, shift = begin // LANES, lax.rem(begin, LANES)
    rows = [order_ref[pl.ds(first + i, 1), :] for i in range(chunks + 1)]
    turn = lax.rem(LANES - shift, LANES)
    near = pltpu.roll(jnp.concatenate(rows[:-1], 0), turn, 1)
    far = pltpu.roll(jnp.concatenate(rows[1:], 0), turn, 1)
    lane = lax.broadcasted_iota(I32, (chunks, LANES), 1)
    index = lax.broadcasted_iota(I32, (chunks, LANES), 0) * LANES + lane
    slots = jnp.where(lane < LANES - shift, near, far)
    return jnp.where(index < width, slots, total)


def select_kernel(axis, share, cap, width, order_ref, raw_ref, *refs):
    outs, full = refs[:-1], refs[-1]
    slots = own_slots(order_ref, width)
    chunks = slots.shape[0]
    full[pl.ds(0, width), :] = raw_ref[...]
    if chunks * LANES > width:
        rest = chunks * LANES - width
        full[pl.ds(width, rest), :] = jnp.zeros((rest, full.shape[1]), BF)
    lane = lambda d: lax.broadcasted_iota(I32, (LANES, LANES), d)
    earlier = jnp.where(lane(0) < lane(1), 1.0, 0.0).astype(BF)
    chunk = lambda d: lax.broadcasted_iota(I32, (chunks, chunks), d)
    above = jnp.where(chunk(1) < chunk(0), 1.0, 0.0).astype(BF)
    buckets = len(outs) if len(outs) > 1 else outs[0].shape[0] // cap

    def bucket(which, store):
        low = which * share
        inside = (slots >= low) & (slots < low + share)
        marks = jnp.where(inside, 1.0, 0.0).astype(BF)
        within = jnp.dot(marks, earlier, preferred_element_type=F32)
        before = jnp.dot(above, marks, preferred_element_type=F32)
        rank = (within + jnp.sum(before, axis=1, keepdims=True)).astype(I32)
        rank = jnp.where(inside, rank, -1)
        row = lax.broadcasted_iota(I32, (cap, LANES), 0)
        hot = jnp.concatenate(
            [
                jnp.where(row == rank[q : q + 1, :], 1.0, 0.0).astype(BF)
                for q in range(chunks)
            ],
            1,
        )
        store(jnp.dot(hot, full[...], preferred_element_type=F32).astype(BF))

    if len(outs) > 1:
        me = lax.axis_index(axis)
        for m, out in enumerate(outs):

            def store(got, out=out):
                out[...] = got

            bucket(m ^ me, store)
    else:

        @pl.loop(0, buckets)
        def _(m):
            def store(got):
                outs[0][pl.ds(pl.multiple_of(m * cap, 16), cap), :] = got

            bucket(m, store)


def select(raw, order, axis, share, cap, buckets, split):
    width, times = raw.shape
    chunks = -(-width // LANES)
    if split:
        shape = [jax.ShapeDtypeStruct((cap, times), BF)] * buckets
    else:
        shape = [jax.ShapeDtypeStruct((buckets * cap, times), BF)]
    return kernel_call(
        functools.partial(select_kernel, axis, share, cap, width),
        12,
        2 * buckets * cap * chunks * LANES * 256,
        2 * (width + buckets * cap) * times,
        out_shape=shape,
        in_specs=[VM, VM],
        out_specs=[VM] * len(shape),
        scratch_shapes=[pltpu.VMEM((chunks * LANES, times), BF)],
    )(order, raw)


def filter_rows(taps_ref, pieces, line, out):
    me = lax.axis_index("row")
    times = pieces[0].shape[1]
    band = toeplitz(taps_ref, times)
    taps = jnp.concatenate([band[:, times:], band[:, :times]], 0)
    high = taps.astype(BF)
    both = jnp.concatenate([high, (taps - high.astype(F32)).astype(BF)], 1)
    rows, block = out.shape[0], line.shape[0]
    line[:, :times] = jnp.zeros((block, times), BF)

    @pl.loop(0, rows // block)
    def _(i):
        there = pl.ds(pl.multiple_of(i * block, block), block)
        for m, piece in enumerate(pieces):
            at = pl.ds(pl.multiple_of(((m ^ me) + 1) * times, times), times)
            line[:, at] = piece[there, :]
        for s in range(len(pieces)):
            got = jnp.dot(
                line[:, s * times : (s + 2) * times], both, preferred_element_type=F32
            )
            got = got[:, :times] + got[:, times:]
            out[there, s * times : (s + 1) * times] = got.astype(out.dtype)


def filter_kernel(taps_ref, *refs):
    pieces, out, line = refs[:-2], refs[-2], refs[-1]
    filter_rows(taps_ref, pieces, line, out)


def filtered(pieces, toep):
    rows, times = pieces[0].shape
    count = len(pieces)
    return kernel_call(
        filter_kernel,
        12,
        8 * rows * count * times * times,
        4 * rows * count * times,
        out_shape=jax.ShapeDtypeStruct((rows, count * times), BF),
        in_specs=[VM] * (1 + count),
        out_specs=VM,
        scratch_shapes=[pltpu.VMEM((row_block(rows), (count + 1) * times), BF)],
    )(toep, *pieces)


def put_rows(list_ref, begin, rows, panel, cap=None):
    group = math.gcd(rows.shape[0], 32 if cap is None else math.gcd(cap, 32))

    @pl.loop(0, rows.shape[0] // group)
    def _(g):
        at = pl.multiple_of(g * group, group)

        def put():
            to = [list_ref[begin + at + q] for q in range(group)]
            values = rows[pl.ds(at, group), :].astype(F32)
            for q in range(group):
                panel[pl.ds(to[q], 1), :] = values[q : q + 1, :]

        if cap is None:
            put()
        else:
            pl.when(list_ref[begin + at] < panel.shape[0] - 8)(put)


def bring(copy):
    copy.start()
    copy.wait()


def ring_source(walk_ref, cols, step):
    return walk_ref[lax.axis_index("col") * cols + step]


def first_place_kernel(steps, cols, cap, rounds_ref, walk_ref, list_ref, extra_ref, *refs):
    nuis, old, _, _ = refs[:4]
    shards, (panel, sem) = refs[4:-2], refs[-2:]

    @pl.when(rounds_ref[0] > 1)
    def _():
        bring(pltpu.make_async_copy(old, panel, sem))

    for step, shard in zip(steps, shards):
        put_rows(list_ref, ring_source(walk_ref, cols, step) * cap, shard, panel, cap)
    put_rows(extra_ref, 0, nuis, panel)


def first_place(shards, steps, rounds, walk, listed, extra, nuis, old, after, cols, cap):
    return kernel_call(
        functools.partial(first_place_kernel, steps, cols, cap),
        6,
        0,
        12 * sum(s.size for s in shards),
        out_shape=jax.ShapeDtypeStruct(old.shape, F32),
        in_specs=[SM, SM, SM, SM, VM, HB, SM, SM] + [VM] * len(shards),
        out_specs=VM,
        scratch_shapes=[pltpu.SemaphoreType.DMA],
    )(rounds, walk, listed, extra, nuis, old, *after, *shards)


def place_kernel(steps, cols, cap, walk_ref, list_ref, *refs):
    shards, panel = refs[: len(steps)], refs[-1]
    for step, shard in zip(steps, shards):
        put_rows(list_ref, ring_source(walk_ref, cols, step) * cap, shard, panel, cap)


def place(shards, steps, walk, listed, panel, cols, cap):
    return kernel_call(
        functools.partial(place_kernel, steps, cols, cap),
        6,
        0,
        12 * sum(s.size for s in shards),
        out_shape=jax.ShapeDtypeStruct(panel.shape, F32),
        in_specs=[SM, SM] + [VM] * (len(shards) + 1),
        out_specs=VM,
        input_output_aliases={2 + len(shards): 0},
    )(walk, listed, *shards, panel)


def halves_kernel(half, up, down, first, second):
    first[...] = up[pl.ds(0, half), :]
    second[...] = down[pl.ds(half, second.shape[0]), :]


def halves_of(up, down, half):
    rows, span = up.shape
    return kernel_call(
        functools.partial(halves_kernel, half),
        3,
        0,
        8 * up.size,
        out_shape=[
            jax.ShapeDtypeStruct((half, span), BF),
            jax.ShapeDtypeStruct((rows - half, span), BF),
        ],
        in_specs=[VM, VM],
        out_specs=[VM, VM],
    )(up, down)


def columns_kernel(part, parts, cap, rounds_ref, list_ref, extra_ref, taps_ref, nuis, old, *refs):
    first, last = part == 0, part == parts - 1
    if last:
        pieces, (out, panel, acc, line, sem) = refs[:-5], refs[-5:]
    else:
        pieces, (panel, acc, line, sem) = refs[:-4], refs[-4:]
    rows = acc.shape[0]
    if first:

        @pl.when(rounds_ref[0] > 1)
        def _():
            bring(pltpu.make_async_copy(old, panel, sem))

    filter_rows(taps_ref, pieces, line, acc)
    put_rows(list_ref, part * rows, acc, panel, cap)
    if first:
        put_rows(extra_ref, 0, nuis, panel)
    if last:
        wide = out.shape[1]
        for at in range(0, wide, LANES):
            size = min(LANES, wide - at)
            out[:, at : at + size] = panel[at : at + size, :].T.astype(BF)


def columns(part, parts, cap, pieces, rounds, listed, extra, nuis, toep, old):
    rows, times = pieces[0].shape
    count = len(pieces)
    high, span = old.shape
    last = part == parts - 1
    outs = [jax.ShapeDtypeStruct((span, high - 8), BF), jax.ShapeDtypeStruct((high, span), F32)]
    held = 4 * rows * span + sum(2 * p.size for p in pieces[4:])
    return kernel_call(
        functools.partial(columns_kernel, part, parts, cap),
        4 + held // MIB,
        8 * rows * span * times,
        12 * rows * span,
        out_shape=outs if last else outs[1],
        in_specs=[SM, SM, SM, VM, VM, HB if part == 0 else VM] + [VM] * count,
        out_specs=[VM, VM] if last else VM,
        input_output_aliases={} if part == 0 else {5: 1 if last else 0},
        scratch_shapes=[
            pltpu.VMEM((rows, span), F32),
            pltpu.VMEM((row_block(rows), span + times), BF),
            pltpu.SemaphoreType.DMA,
        ],
    )(rounds, listed, extra, toep, nuis, old, *pieces)


def update_kernel(begins, step, cols, cap, block, parts, walk_ref, list_ref, *refs):
    shards, refs = refs[: len(begins)], refs[len(begins) :]
    weights, priors, (_, out, panel, held, sems) = refs[0], refs[1 : 1 + parts], refs[1 + parts :]
    source = ring_source(walk_ref, cols, step) * cap
    for begin, shard in zip(begins, shards):
        put_rows(list_ref, source + begin, shard, panel, math.gcd(cap, shard.shape[0]))
    slots, wide = held.shape[0], held.shape[2]
    each = priors[0].shape[0] // block

    def drain(i, slot):
        there = out.at[pl.ds(pl.multiple_of(i * block, 8), block), :]
        return pltpu.make_async_copy(held.at[slot], there, sems.at[slot])

    for part, prior in enumerate(priors):

        @pl.loop(part * each, (part + 1) * each)
        def _(i, part=part, prior=prior):
            slot = lax.rem(i, slots)

            @pl.when(i >= slots)
            def _():
                drain(i - slots, slot).wait()

            rows = panel[pl.ds(pl.multiple_of(i * block, 8), block), :].astype(BF)
            at = pl.ds(pl.multiple_of((i - part * each) * block, 8), block)
            for begin in range(0, wide, 2 * LANES):
                tile = pl.ds(begin, min(2 * LANES, wide - begin))
                got = jnp.dot(rows, weights[:, tile], preferred_element_type=F32)
                held[slot, :, tile] = prior[at, tile] + got
            drain(i, slot).start()

    steps = each * parts
    for i in range(max(0, steps - slots), steps):
        drain(i, i % slots).wait()


def update(shards, begins, step, walk, listed, panel, weights, priors, cols, cap):
    part, wide = priors[0].shape
    parts, span = len(priors), weights.shape[0]
    high = part * parts
    block = max(b for b in range(16, 257, 16) if part % b == 0)
    slots = min(3, high // block)
    count = len(shards)
    return kernel_call(
        functools.partial(update_kernel, begins, step, cols, cap, block, parts),
        12,
        2 * high * wide * span,
        8 * high * wide,
        out_shape=[
            jax.ShapeDtypeStruct((high, wide), F32),
            jax.ShapeDtypeStruct(panel.shape, F32),
        ],
        in_specs=[SM, SM] + [VM] * (count + 2 + parts),
        out_specs=[HB, VM],
        input_output_aliases={3 + parts + count: 1},
        scratch_shapes=[
            pltpu.VMEM((slots, block, wide), F32),
            pltpu.SemaphoreType.DMA((slots,)),
        ],
    )(walk, listed, *shards, weights, *priors, panel)[0]


def nuisance_kernel(taps_ref, *refs):
    pieces, out, acc = refs[:-2], refs[-2], refs[-1]
    me = lax.axis_index("row")
    lines, times = pieces[0].shape
    count, params = out.shape[0], lines - 1
    band = toeplitz(taps_ref, times)
    column = lax.broadcasted_iota(I32, (count, times), 0)
    owner = (column // params).astype(F32)
    acc[...] = jnp.zeros_like(acc)
    for m, piece in enumerate(pieces):
        picked = jnp.zeros((count, times), F32)
        for q in range(params):
            picked = jnp.where(lax.rem(column, params) == q, piece[q : q + 1, :], picked)
        raw = jnp.where(piece[params:lines, :] == owner, picked, 0.0)
        got = jnp.dot(
            raw, band, precision=lax.Precision.HIGHEST, preferred_element_type=F32
        )
        at = pl.ds(pl.multiple_of((m ^ me) * times, times), 2 * times)
        acc[:, at] = acc[:, at] + got
    out[...] = acc[:, : out.shape[1]].astype(BF).astype(F32)


def filtered_nuisance(pieces, toep, count):
    groups = len(pieces)
    times = pieces[0].shape[1]
    return kernel_call(
        nuisance_kernel,
        8,
        24 * groups * count * times * times,
        4 * count * groups * times,
        out_shape=jax.ShapeDtypeStruct((count, groups * times), F32),
        in_specs=[VM] * (1 + groups),
        out_specs=VM,
        scratch_shapes=[pltpu.VMEM((count, (groups + 1) * times), F32)],
    )(toep, *pieces)


def keys_kernel(bits, shares, caps, slots_ref, keys, rounds):
    slots = slots_ref[...]
    groups, width = slots.shape
    key = (lax.broadcasted_iota(I32, slots.shape, 1) << bits) | slots
    need = jnp.int32(1)
    for i, (axis, share, cap) in enumerate(zip(("row", "col"), shares, caps)):
        low = lax.axis_index(axis) * share
        inside = (slots >= low) & (slots < low + share)
        keys[i * groups : (i + 1) * groups, :] = jnp.where(inside, key, width << bits)
        most = jnp.zeros((groups, 1), F32)
        for b in range(lax.axis_size(axis)):
            mark = (slots >= b * share) & (slots < (b + 1) * share)
            found = jnp.sum(jnp.where(mark, 1.0, 0.0), axis=1, keepdims=True)
            most = jnp.maximum(most, found)
        need = jnp.maximum(need, (jnp.max(most).astype(I32) + cap - 1) // cap)
    rounds[0] = need


def overflow_round(step, raw, slots, toep, sizes, panels):
    (row_share, cap_row), (col_share, cap_col) = sizes
    times = raw.shape[1]
    rows, cols = lax.axis_size("row"), lax.axis_size("col")
    r, c = lax.axis_index("row"), lax.axis_index("col")
    own = slots[c]

    def buckets(share, cap, groups):
        owner = own // share
        hit = owner == jnp.arange(groups)[:, None]
        rank = jnp.sum(jnp.where(hit, jnp.cumsum(hit.astype(I32), axis=1), 0), axis=0) - 1
        rank = rank - step * cap
        to = jnp.where((rank >= 0) & (rank < cap), owner * cap + rank, -1)
        hot = (jnp.arange(groups * cap)[:, None] == to[None, :]).astype(BF)
        got = jnp.dot(hot, raw, preferred_element_type=F32).astype(BF)
        return got.reshape(groups, cap, times)

    def listing(share, cap, index):
        hit = slots // share == index
        rank = jnp.cumsum(hit.astype(I32), axis=1) - 1
        to = jnp.where(hit, rank - step * cap, -1)
        hot = to[:, None, :] == jnp.arange(cap)[None, :, None]
        code = jnp.where(hot, slots[:, None, :] - index * share + 1, 0)
        found = jnp.sum(code, axis=2)
        return jnp.where(found > 0, found - 1, share)

    def filter_all(x):
        return filtered([lax.dynamic_index_in_dim(x, m ^ r, 0, False) for m in range(rows)], toep)

    def everywhere(x, axis):
        size = lax.axis_size(axis)
        return lax.all_to_all(jnp.broadcast_to(x[None], (size,) + x.shape), axis, 0, 0, tiled=True)

    got = lax.all_to_all(buckets(row_share, cap_row, rows), "row", 0, 0, tiled=True)
    shards = everywhere(filter_all(got), "col")
    held = lax.all_to_all(buckets(col_share, cap_col, cols), "col", 0, 0, tiled=True)
    held = filter_all(everywhere(held.reshape(cols * cap_col, times), "row"))
    row_list = listing(row_share, cap_row, r).reshape(-1)
    col_list = listing(col_share, cap_col, c).reshape(-1)
    span = held.shape[1]
    return (
        panels[0].at[row_list].set(shards.reshape(-1, span).astype(F32)),
        panels[1].at[col_list].set(held.astype(F32)),
    )


def per_device(design, nuisance_vals, arc_index, filter_taps, ordering, normal_prior):
    times, width = design.shape
    rows, cols = lax.axis_size("row"), lax.axis_size("col")
    total = ordering.shape[0]
    row_share, col_share = total // rows, total // cols
    span = rows * times
    extras = total - width * cols
    cap_row, cap_col = capacity(width, rows), capacity(width, cols)

    raw = design.T
    order2d = ordering.reshape(total // LANES, LANES)
    to_rows = select(raw, order2d, "row", row_share, cap_row, rows, True)
    pieces = [to_rows[0]] + [swapped(to_rows[m], "row", m) for m in range(1, rows)]
    late, _ = lax.optimization_barrier((raw, to_rows[-1]))
    (to_cols,) = select(late, order2d, "col", col_share, cap_col, cols, False)
    toep = filter_taps.reshape(1, -1)
    *pieces, _ = lax.optimization_barrier((*pieces, to_cols))
    shard = filtered(pieces, toep)
    to_cols, _ = lax.optimization_barrier((to_cols, shard))
    mine = lax.all_to_all(to_cols, "col", 0, 0, tiled=True)

    params = jnp.concatenate([nuisance_vals, arc_index.astype(F32)[None]], 0)
    params, _ = lax.optimization_barrier((params, shard))
    params = [params] + [swapped(params, "row", m) for m in range(1, rows)]
    ordering, _ = lax.optimization_barrier((ordering, shard))
    slots = ordering[: width * cols].reshape(cols, width)
    bits = (total - 1).bit_length()
    keys, rounds = kernel_call(
        functools.partial(
            keys_kernel, bits, (row_share, col_share), (cap_row, cap_col)
        ),
        4,
        0,
        12 * width * cols,
        out_shape=[
            jax.ShapeDtypeStruct((2 * cols, width), I32),
            jax.ShapeDtypeStruct((1,), I32),
        ],
        in_specs=[VM],
        out_specs=[VM, SM],
    )(slots)
    order = ring_order(cols)
    ahead = [(order[i], order[(i + 1) % cols]) for i in range(cols)]
    back = [(b, a) for a, b in ahead]
    walk = jnp.array(
        [order[(order.index(i) + j) % cols] for i in range(cols) for j in range(cols)], I32
    )

    up = lax.ppermute(shard, "col", ahead)
    down = lax.ppermute(shard, "col", back)
    keys = lax.sort(keys, dimension=1)
    low_row = (lax.axis_index("row") * row_share).astype(I32)
    low_col = (lax.axis_index("col") * col_share).astype(I32)

    def listing(part, low, share, cap):
        part = part[:, :cap]
        found = (part & ((1 << bits) - 1)) - low
        return jnp.where(part < (width << bits), found, share).reshape(-1)

    row_list = listing(keys[:cols], low_row, row_share, cap_row)
    col_list = listing(keys[cols:], low_col, col_share, cap_col)

    def extra_list(low, share):
        at = ordering[width * cols :] - low
        return jnp.where((at >= 0) & (at < share), at, share)

    nuis = filtered_nuisance(params, toep, extras)

    shapes = [(row_share + 8, span), (col_share + 8, span)]
    empty = kernel_call(
        lambda *refs: None,
        1,
        0,
        0,
        out_shape=[jax.ShapeDtypeStruct(s, F32) for s in shapes],
        out_specs=[HB, HB],
    )()
    sizes = ((row_share, cap_row), (col_share, cap_col))

    def more(carry):
        return carry[0] < rounds[0]

    def again(carry):
        step, *panels = carry
        panels = overflow_round(step, raw, slots, toep, sizes, panels)
        return (step + 1, *panels)

    _, old_rows, old_cols = lax.while_loop(more, again, (jnp.int32(1), *empty))

    split = [{0: piece} for piece in halves_of(mine, mine, mine.shape[0] // 2)]
    distance = rows // 2
    while distance:
        for m in list(split[0]):
            for parts in split:
                parts[m ^ distance] = swapped(parts[m], "row", distance)
        distance //= 2

    steps, half = cols // 2, cap_row // 2
    half -= half % 16
    row_extra = extra_list(low_row, row_share)
    col_extra = extra_list(low_col, col_share)

    def column_part(part, panel):
        pieces = [split[part][m] for m in range(rows)]
        return columns(
            part, 2, cap_col, pieces, rounds, col_list, col_extra, nuis, toep, panel
        )

    panel = None
    batch, at = [], []
    for i in range(1, steps):
        if i > 1:
            up = lax.ppermute(up, "col", ahead)
            down = lax.ppermute(down, "col", back)
            if panel is None:
                panel = first_place(
                    [shard],
                    [0],
                    rounds,
                    walk,
                    row_list,
                    row_extra,
                    nuis,
                    old_rows,
                    (col_list, col_extra),
                    cols,
                    cap_row,
                )
            else:
                for j in range(0, len(batch), 2):
                    panel = place(
                        batch[j : j + 2], at[j : j + 2], walk, row_list, panel, cols, cap_row
                    )
                batch, at = [], []
        batch += [up, down]
        at += [(cols - i) % cols, i]
    col_panel = column_part(0, old_cols)
    up, down = halves_of(up, down, half)
    up = lax.ppermute(up, "col", ahead)
    down = lax.ppermute(down, "col", back)
    panel = place(batch, at, walk, row_list, panel, cols, cap_row)
    weights, _ = column_part(1, col_panel)
    return update(
        [up, down],
        (0, half),
        steps,
        walk,
        row_list,
        panel,
        weights,
        [normal_prior],
        cols,
        cap_row,
    )


def solution(mesh):
    return jax.shard_map(
        per_device,
        mesh=mesh,
        in_specs=(P("row", "col"), P(None, "row"), P("row"), P(), P(), P("row", "col")),
        out_specs=P("row", "col"),
        check_vma=False,
    )
```
